128 devices in a mesh: ctx: 8 (over z, x_hi), tp: 16 (over x_lo, y, core).
Axes of the slice: x: 4 (x_hi: 2, x_lo: 2; x = x_hi * 2 + x_lo), y: 4, z: 4, core: 2. Of those that a mesh axis runs over, the one named last changes fastest.
Arguments:
- residual_in: bfloat16 [1024, 8192], P('ctx', 'tp'), may hold values from -0.3 to 0.3
- dh_rest: bfloat16 [1024, 8192], P('ctx', 'tp'), may hold values from -0.29882812 to 0.29882812
- w_query: bfloat16 [8192, 8192], P(None, 'tp'), may hold values from -0.0625 to 0.0625
- w_key: bfloat16 [8192, 1024], P(None, 'tp'), may hold values from -0.0625 to 0.0625
- w_value: bfloat16 [8192, 1024], P(None, 'tp'), may hold values from -0.0625 to 0.0625
- q_raw: bfloat16 [1024, 8192], P('ctx', 'tp'), may hold values from -33 to 33
- k_raw: bfloat16 [1024, 1024], P('ctx'), may hold values from -33 to 33
- v_win: bfloat16 [1024, 1024], P('ctx'), may hold values from -6 to 6
- cache_k: bfloat16 [8192, 1024], P('ctx'), may hold values from -90 to 90
- cache_v: bfloat16 [8192, 1024], P('ctx'), may hold values from -6 to 6
- d_attn: bfloat16 [1024, 8192], P('ctx', 'tp'), may hold values from -6 to 6
- s_qk: float32 [128], replicated, may hold values from 0.8 to 5.5
- cache_live: int32 [1], replicated, may hold values from 4096 to 8192
Outputs:
- grad_input: float32 [1024, 8192], P('ctx', 'tp')
The draws below stay inside these ranges and needn't reach their ends.
All inputs are finite; a program needn't handle non-finite values.
Results may differ from the reference program's by a relative error of at most 0.0025.
The reference program's roundings to bfloat16 on the way count: a program that leaves them out, or rounds other values in their place, can miss the bound.
Values may be sent and summed in bfloat16 or wider, within the bound.
No kernel may reach another device: no remote copies, remote signals or barrier semaphores. Data moves between devices by JAX's collectives and lax.ppermute only.
A program may use at most 128 MiB of HBM per device.

```python
import math
import jax
import jax.numpy as jnp
from jax import lax

D = 8192
H = 64
KVH = 8
HD = 128
GROUP = 8
TOKENS = 1024
CACHE = 8192


def rough_heads(key, rows, heads, base):
    noise = jnp.clip(jax.random.normal(jax.random.fold_in(key, 1), (rows, heads, HD), jnp.float32), -6.0, 6.0)
    row_scale = jnp.exp(jax.random.uniform(jax.random.fold_in(key, 2), (rows, heads, 1), jnp.float32) * math.log(10.0))
    col_scale = jnp.exp(jax.random.uniform(jax.random.fold_in(key, 3), (1, 1, HD), jnp.float32) * math.log(10.0))
    return (noise * row_scale * col_scale * base).reshape(rows, heads * HD)


def window_keys(key):
    raw = rough_heads(jax.random.fold_in(key, 101), TOKENS, KVH, 0.05)
    return raw


def draw_k_raw(key, part):
    return window_keys(key).astype(jnp.bfloat16)


def draw_q_raw(key, part):
    raw = rough_heads(jax.random.fold_in(key, 202), TOKENS, H, 0.05)
    return raw.astype(jnp.bfloat16)


def draw_cache_k(key, part):
    raw = rough_heads(jax.random.fold_in(key, 303), CACHE, KVH, 0.05)
    return raw.astype(jnp.bfloat16)


def draw_residual_in(key, part):
    row_scale = jnp.exp(jax.random.uniform(jax.random.fold_in(key, 41), (TOKENS, 1), jnp.float32) * math.log(10.0))
    col_scale = jnp.exp(jax.random.uniform(jax.random.fold_in(key, 42), (1, D), jnp.float32) * math.log(10.0))
    noise = jnp.clip(jax.random.normal(jax.random.fold_in(key, 45), (TOKENS, D), jnp.float32), -6.0, 6.0)
    return (noise * row_scale * col_scale * 0.0005).astype(jnp.bfloat16)


def draw_s_qk(key, part):
    return jax.random.uniform(jax.random.fold_in(key, 52), (HD,), jnp.float32, 0.8, 1.25)


def block_scale(key, shape, pieces, smallest, top_value):
    def one(position, blocks):
        heights = jax.random.uniform(jax.random.fold_in(jax.random.fold_in(key, 6), position), (blocks,), jnp.float32, smallest / len(pieces), top_value / len(pieces))
        return jnp.repeat(jnp.exp(heights), shape[position] // blocks).reshape((-1,) + (1,) * (len(shape) - position - 1))

    factor_of = one(*pieces[0])
    for cut in pieces[1:]:
        factor_of = factor_of * one(*cut)
    return factor_of


def gaussian(rng, dims, scale, limit, cuts=(), kind=jnp.bfloat16):
    drawn = scale * jax.random.normal(rng, dims, jnp.float32)
    if cuts:
        drawn = drawn * block_scale(rng, dims, cuts, -0.22, 0.18)
    return jnp.clip(drawn, -limit, limit).astype(kind)


def setup_inputs(seed: int = 0) -> dict:
    streams_of = jax.random.split(jax.random.key(seed), 14)
    return {
        "residual_in": draw_residual_in(jax.random.fold_in(streams_of[13], 71), 0),
        "dh_rest": gaussian(streams_of[1], (TOKENS, D), 0.05, 0.29882812, ((0, 8), (1, 16))),
        "w_query": gaussian(streams_of[2], (D, H * HD), D ** -0.5, 0.0625, ((1, 16),)),
        "w_key": gaussian(streams_of[3], (D, KVH * HD), D ** -0.5, 0.0625, ((1, 16),)),
        "w_value": gaussian(streams_of[4], (D, KVH * HD), D ** -0.5, 0.0625, ((1, 16),)),
        "q_raw": draw_q_raw(jax.random.fold_in(streams_of[13], 71), 0),
        "k_raw": draw_k_raw(jax.random.fold_in(streams_of[13], 71), 0),
        "v_win": gaussian(streams_of[7], (TOKENS, KVH * HD), 1.0, 6.0, ((0, 8),)),
        "cache_k": draw_cache_k(jax.random.fold_in(streams_of[13], 71), 0),
        "cache_v": gaussian(streams_of[9], (CACHE, KVH * HD), 1.0, 6.0, ((0, 8),)),
        "d_attn": gaussian(streams_of[10], (TOKENS, H * HD), 1.0, 6.0, ((0, 8), (1, 16))),
        "s_qk": draw_s_qk(jax.random.fold_in(streams_of[13], 71), 0),
        "cache_live": jax.random.randint(streams_of[12], (1,), CACHE // 2, CACHE + 1).astype(jnp.int32),
    }


EPS = 1e-06

def unit_rows(values, qk_gain):
    width = values.shape[-1]
    mean_sq = lax.optimization_barrier(jnp.mean(values * values, axis=-1, keepdims=True))
    return values * (lax.rsqrt(mean_sq + EPS) / math.sqrt(width)) * qk_gain

def unit_back(values, qk_gain, grad):
    width = values.shape[-1]
    mean_sq = lax.optimization_barrier(jnp.mean(values * values, axis=-1, keepdims=True))
    factor = lax.rsqrt(mean_sq + EPS) / math.sqrt(width)
    weighted = qk_gain * grad
    inner = lax.optimization_barrier(jnp.sum(weighted * values, axis=-1, keepdims=True))
    return factor * (weighted - values * inner / (width * (mean_sq + EPS)))

def reference(residual_in, dh_rest, w_query, w_key, w_value, q_raw, k_raw, v_win, cache_k, cache_v, d_attn, s_qk, cache_live):
    score_scale = math.sqrt(HD)
    query_raw = q_raw.astype(jnp.float32).reshape(TOKENS, H, HD)
    query_norm = unit_rows(query_raw, s_qk).astype(jnp.bfloat16)
    key_raw = k_raw.astype(jnp.float32).reshape(TOKENS, KVH, HD)
    key_window = unit_rows(key_raw, s_qk).astype(jnp.bfloat16)
    key_cache = unit_rows(cache_k.astype(jnp.float32).reshape(CACHE, KVH, HD), s_qk).astype(jnp.bfloat16)
    keys_all = jnp.concatenate([key_cache, key_window], 0).transpose(1, 0, 2)
    values_all = jnp.concatenate([cache_v, v_win], 0).reshape(CACHE + TOKENS, KVH, HD).transpose(1, 0, 2)
    key_pos = jnp.arange(CACHE + TOKENS, dtype=jnp.int32)
    query_pos = CACHE + jnp.arange(TOKENS, dtype=jnp.int32)
    visible = (key_pos[None, :] >= CACHE - cache_live[0]) & (key_pos[None, :] <= query_pos[:, None])
    heads_query = query_norm.transpose(1, 0, 2)
    heads_dout = d_attn.reshape(TOKENS, H, HD).transpose(1, 0, 2)
    head_ids = jnp.arange(H, dtype=jnp.int32)

    def one_head(inputs):
        query, dout, head = inputs
        keys = lax.dynamic_index_in_dim(keys_all, head // GROUP, 0, keepdims=False)
        values = lax.dynamic_index_in_dim(values_all, head // GROUP, 0, keepdims=False)
        scores = jnp.dot(query, keys.T, preferred_element_type=jnp.float32) * score_scale
        row_max = lax.optimization_barrier(jnp.max(jnp.where(visible, scores, -1e+30), axis=1, keepdims=True))
        expo = jnp.where(visible, jnp.exp(scores - row_max), 0.0)
        lse = row_max + jnp.log(lax.optimization_barrier(jnp.sum(expo, axis=1, keepdims=True)))
        probs = jnp.where(visible, jnp.exp(scores - lse), 0.0)
        dprobs = jnp.dot(dout, values.T, preferred_element_type=jnp.float32)
        delta = lax.optimization_barrier(jnp.sum(probs * dprobs, axis=1, keepdims=True))
        dscores = (probs * (dprobs - delta)).astype(jnp.bfloat16)
        probs_low = probs.astype(jnp.bfloat16)
        dqn = jnp.dot(dscores, keys, preferred_element_type=jnp.float32) * score_scale
        dkn = jnp.dot(dscores[:, CACHE:].T, query, preferred_element_type=jnp.float32) * score_scale
        dvn = jnp.dot(probs_low[:, CACHE:].T, dout, preferred_element_type=jnp.float32)
        return (dqn, dkn, dvn)
    dqn, dkn, dvn = lax.map(one_head, (heads_query, heads_dout, head_ids))
    dkn_sum = lax.optimization_barrier(jnp.sum(dkn.reshape(KVH, GROUP, TOKENS, HD), axis=1)).transpose(1, 0, 2)
    dvn_sum = lax.optimization_barrier(jnp.sum(dvn.reshape(KVH, GROUP, TOKENS, HD), axis=1)).transpose(1, 0, 2)
    grad_q = unit_back(query_raw, s_qk, dqn.transpose(1, 0, 2)).astype(jnp.bfloat16).reshape(TOKENS, H * HD)
    grad_k = unit_back(key_raw, s_qk, dkn_sum).astype(jnp.bfloat16).reshape(TOKENS, KVH * HD)
    grad_v = dvn_sum.astype(jnp.bfloat16).reshape(TOKENS, KVH * HD)
    grad_x = jnp.dot(grad_q, w_query.T, preferred_element_type=jnp.float32)
    grad_x = grad_x + jnp.dot(grad_k, w_key.T, preferred_element_type=jnp.float32)
    grad_x = grad_x + jnp.dot(grad_v, w_value.T, preferred_element_type=jnp.float32)
    grad_total = grad_x + dh_rest.astype(jnp.float32)
    return unit_back(residual_in.astype(jnp.float32), 1.0, grad_total)
```

```python
import functools
import math

import jax
import jax.numpy as jnp
from jax import lax
from jax.experimental import pallas as pl
from jax.experimental.pallas import tpu as pltpu
from jax.sharding import Mesh
from jax.sharding import PartitionSpec as P

D = 8192
KVH = 8
HD = 128
CACHE = 8192
TOKENS = 1024
KEYS = CACHE + TOKENS
CTX = 8
TOK = TOKENS // CTX
HEADS = 4
ROWS = HEADS * TOK
HALF_CACHE = CACHE // CTX // 2
HALF_WIN = TOK // 2
HALF = HALF_CACHE + HALF_WIN
CUT = HALF // 2
KB = 512
CACHE_BLOCKS = CACHE // KB
WIN_BLOCKS = TOKENS // KB
EPS = 1e-06
SCALE = math.sqrt(HD)
EXP_SCALE = SCALE * math.log2(math.e)
NEG = -1e30
VMEM_LIMIT = 56 * 1024 * 1024
TP_AXES = ("xl", "y", "c")
CTX_AXES = ("z", "xh")
CHIP_AXES = ("xl", "y")


def contract_last(left, right):
    return lax.dot_general(
        left, right, (((1,), (1,)), ((), ())), preferred_element_type=jnp.float32
    )


def contract_first(left, right):
    return lax.dot_general(
        left, right, (((0,), (0,)), ((), ())), preferred_element_type=jnp.float32
    )


def unit_rows(values, qk_gain):
    width = values.shape[-1]
    mean_sq = jnp.mean(values * values, axis=-1, keepdims=True)
    return values * (lax.rsqrt(mean_sq + EPS) / math.sqrt(width)) * qk_gain


def unit_back(values, qk_gain, grad):
    width = values.shape[-1]
    mean_sq = jnp.mean(values * values, axis=-1, keepdims=True)
    factor = lax.rsqrt(mean_sq + EPS) / math.sqrt(width)
    weighted = qk_gain * grad
    inner = jnp.sum(weighted * values, axis=-1, keepdims=True)
    return factor * (weighted - values * inner / (width * (mean_sq + EPS)))


def head_cols(h):
    return slice(h * HD, (h + 1) * HD)


def head_rows(h):
    return slice(h * TOK, (h + 1) * TOK)


def pack_kernel(idx_ref, ck_ref, cv_ref, kr_ref, vw_ref, gain_ref, out_ref):
    gain = gain_ref[...]
    out_ref[:HALF_CACHE, :HD] = unit_rows(ck_ref[...].astype(jnp.float32), gain).astype(
        jnp.bfloat16
    )
    out_ref[:HALF_CACHE, HD:] = cv_ref[...]
    out_ref[HALF_CACHE:, :HD] = unit_rows(kr_ref[...].astype(jnp.float32), gain).astype(
        jnp.bfloat16
    )
    out_ref[HALF_CACHE:, HD:] = vw_ref[...]


def pack_rows(idx, cache_k, cache_v, k_raw, v_win, gain):
    def at(i, idx):
        return (idx[1], idx[0])

    return pl.pallas_call(
        pack_kernel,
        out_shape=jax.ShapeDtypeStruct((HALF, 2 * HD), jnp.bfloat16),
        grid_spec=pltpu.PrefetchScalarGridSpec(
            num_scalar_prefetch=1,
            grid=(1,),
            in_specs=[
                pl.BlockSpec((HALF_CACHE, HD), at),
                pl.BlockSpec((HALF_CACHE, HD), at),
                pl.BlockSpec((HALF_WIN, HD), at),
                pl.BlockSpec((HALF_WIN, HD), at),
                pl.BlockSpec((1, HD), lambda i, idx: (0, 0)),
            ],
            out_specs=pl.BlockSpec((HALF, 2 * HD), lambda i, idx: (0, 0)),
        ),
        name="pack_rows",
    )(idx, cache_k, cache_v, k_raw, v_win, gain)


def visible_mask(info_ref, start):
    kpos = start + lax.broadcasted_iota(jnp.int32, (ROWS, KB), 1)
    qpos = (
        CACHE
        + info_ref[9] * TOK
        + lax.rem(lax.broadcasted_iota(jnp.int32, (ROWS, KB), 0), jnp.int32(TOK))
    )
    return (kpos >= info_ref[8]) & (kpos <= qpos)


def stack_rows(src_ref, dst_ref):
    for h in range(HEADS):
        dst_ref[head_rows(h), :] = src_ref[:, head_cols(h)]


def block_pair(info_ref, q_s, do_s, k_ref, v_ref, b):
    start = pl.multiple_of(b * KB, KB)
    keys = k_ref[pl.ds(start, KB), :]
    scores = contract_last(q_s[...], keys)
    dprobs = contract_last(do_s[...], v_ref[pl.ds(start, KB), :])
    return start, keys, scores, dprobs


def grads_block(info_ref, q_s, do_s, k_ref, v_ref, lse_ref, delta_ref, b, masked):
    start, keys, scores, dprobs = block_pair(info_ref, q_s, do_s, k_ref, v_ref, b)
    lse = lse_ref[...]
    delta = delta_ref[...]
    probs = []
    dscores = []
    mask = visible_mask(info_ref, start) if masked else None
    for g in range(KB // HD):
        cols = head_cols(g)
        p = jnp.exp2(scores[:, cols] * EXP_SCALE - lse)
        if masked:
            p = jnp.where(mask[:, cols], p, 0.0)
            probs.append(p.astype(jnp.bfloat16))
        dscores.append((p * (dprobs[:, cols] - delta)).astype(jnp.bfloat16))
    dscores = jnp.concatenate(dscores, 1)
    probs = jnp.concatenate(probs, 1) if masked else None
    return start, keys, probs, dscores


def stats_kernel(info_ref, *refs):
    pieces = refs[:20]
    q_ref, do_ref, gain_ref = refs[20:23]
    k_ref, v_ref, lse_ref, delta_ref, dq_ref, dkv_ref = refs[23:29]
    q_s, do_s, m_s, l_s, w_s = refs[29:]
    core = info_ref[10]

    def place(piece, source, half, first):
        rows = piece.shape[0]
        cache_rows = min(rows, HALF_CACHE - first)
        at = pl.multiple_of(source * (2 * HALF_CACHE) + half * HALF_CACHE + first, 32)
        k_ref[pl.ds(at, cache_rows), :] = piece[:cache_rows, :HD]
        v_ref[pl.ds(at, cache_rows), :] = piece[:cache_rows, HD:]
        if rows > cache_rows:
            at = pl.multiple_of(CACHE + source * TOK + half * HALF_WIN, HALF_WIN)
            k_ref[pl.ds(at, HALF_WIN), :] = piece[cache_rows:, :HD]
            v_ref[pl.ds(at, HALF_WIN), :] = piece[cache_rows:, HD:]

    for side in range(2):
        half = core if side == 0 else 1 - core
        part = pieces[side * 10 : side * 10 + 10]
        for n in range(6):
            place(part[n], info_ref[n], half, 0)
        for n in range(2):
            place(part[6 + 2 * n], info_ref[6 + n], half, 0)
            place(part[7 + 2 * n], info_ref[6 + n], half, CUT)

    gain = gain_ref[...]
    for h in range(HEADS):
        raw = q_ref[:, head_cols(h)].astype(jnp.float32)
        q_s[head_rows(h), :] = unit_rows(raw, gain).astype(jnp.bfloat16)
    stack_rows(do_ref, do_s)
    m_s[...] = jnp.full((ROWS, HD), NEG, jnp.float32)
    l_s[...] = jnp.zeros((ROWS, HD), jnp.float32)
    w_s[...] = jnp.zeros((ROWS, HD), jnp.float32)

    def stat_block(b, masked):
        start, _, scores, dprobs = block_pair(info_ref, q_s, do_s, k_ref, v_ref, b)
        if masked:
            mask = visible_mask(info_ref, start)
            scores = jnp.where(mask, scores, NEG)
        old = m_s[...]
        top = old
        for g in range(KB // HD):
            top = jnp.maximum(top, scores[:, head_cols(g)])
        keep = jnp.exp2((old - top) * EXP_SCALE)
        total = l_s[...] * keep
        weighted = w_s[...] * keep
        for g in range(KB // HD):
            e = jnp.exp2((scores[:, head_cols(g)] - top) * EXP_SCALE)
            if masked:
                e = jnp.where(mask[:, head_cols(g)], e, 0.0)
            total = total + e
            weighted = weighted + e * dprobs[:, head_cols(g)]
        m_s[...] = top
        l_s[...] = total
        w_s[...] = weighted

    first = info_ref[8] // KB
    win_blocks = info_ref[9] * TOK // KB + 1
    stat_block(first, True)

    @pl.loop(first + 1, CACHE_BLOCKS)
    def _(b):
        stat_block(b, False)

    @pl.loop(CACHE_BLOCKS, CACHE_BLOCKS + win_blocks)
    def _(b):
        stat_block(b, True)

    row_max = jnp.max(m_s[...], axis=1, keepdims=True)
    fix = jnp.exp2((m_s[...] - row_max) * EXP_SCALE)
    total = jnp.sum(l_s[...] * fix, axis=1, keepdims=True)
    weighted = jnp.sum(w_s[...] * fix, axis=1, keepdims=True)
    lse = row_max * EXP_SCALE + jnp.log2(total)
    lse_ref[...] = jnp.broadcast_to(lse, (ROWS, HD))
    delta_ref[...] = jnp.broadcast_to(weighted / total, (ROWS, HD))
    dq_ref[...] = jnp.zeros((ROWS, HD), jnp.float32)
    dkv_ref[...] = jnp.zeros((TOKENS, 2 * HD), jnp.float32)

    @pl.loop(0, win_blocks)
    def _(w):
        start, keys, probs, dscores = grads_block(
            info_ref, q_s, do_s, k_ref, v_ref, lse_ref, delta_ref, CACHE_BLOCKS + w, True
        )
        dq_ref[...] += jnp.dot(dscores, keys, preferred_element_type=jnp.float32)
        at = pl.multiple_of(w * KB, KB)
        dkv_ref[pl.ds(at, KB), :HD] = contract_first(dscores, q_s[...]) * SCALE
        dkv_ref[pl.ds(at, KB), HD:] = contract_first(probs, do_s[...])


def stats_call(info, pieces, q_raw, d_attn, gain):
    shape = jax.ShapeDtypeStruct
    return pl.pallas_call(
        stats_kernel,
        out_shape=(
            shape((KEYS, HD), jnp.bfloat16),
            shape((KEYS, HD), jnp.bfloat16),
            shape((ROWS, HD), jnp.float32),
            shape((ROWS, HD), jnp.float32),
            shape((ROWS, HD), jnp.float32),
            shape((TOKENS, 2 * HD), jnp.float32),
        ),
        in_specs=[pl.BlockSpec(memory_space=pltpu.SMEM)]
        + [pl.BlockSpec(memory_space=pltpu.VMEM)] * 23,
        out_specs=[pl.BlockSpec(memory_space=pltpu.VMEM)] * 6,
        scratch_shapes=[
            pltpu.VMEM((ROWS, HD), jnp.bfloat16),
            pltpu.VMEM((ROWS, HD), jnp.bfloat16),
            pltpu.VMEM((ROWS, HD), jnp.float32),
            pltpu.VMEM((ROWS, HD), jnp.float32),
            pltpu.VMEM((ROWS, HD), jnp.float32),
        ],
        compiler_params=pltpu.CompilerParams(vmem_limit_bytes=VMEM_LIMIT),
        name="attn_stats",
    )(info, *pieces, q_raw, d_attn, gain)


def cache_kernel(
    info_ref,
    k_ref,
    v_ref,
    lse_ref,
    delta_ref,
    dq_in,
    q_ref,
    do_ref,
    gain_ref,
    out_ref,
    q_s,
    do_s,
    dq_s,
):
    gain = gain_ref[...]
    for h in range(HEADS):
        raw = q_ref[:, head_cols(h)].astype(jnp.float32)
        q_s[head_rows(h), :] = unit_rows(raw, gain).astype(jnp.bfloat16)
    stack_rows(do_ref, do_s)
    dq_s[...] = dq_in[...]

    def step(b, masked):
        _, keys, _, dscores = grads_block(
            info_ref, q_s, do_s, k_ref, v_ref, lse_ref, delta_ref, b, masked
        )
        dq_s[...] += jnp.dot(dscores, keys, preferred_element_type=jnp.float32)

    first = info_ref[8] // KB
    step(first, True)

    @pl.loop(first + 1, CACHE_BLOCKS)
    def _(b):
        step(b, False)

    for h in range(HEADS):
        raw = q_ref[:, head_cols(h)].astype(jnp.float32)
        grad = unit_back(raw, gain, dq_s[head_rows(h), :] * SCALE)
        out_ref[:, head_cols(h)] = grad.astype(jnp.bfloat16)


def cache_call(info, keys, values, lse, delta, dq, q_raw, d_attn, gain):
    return pl.pallas_call(
        cache_kernel,
        out_shape=jax.ShapeDtypeStruct((TOK, HEADS * HD), jnp.bfloat16),
        in_specs=[pl.BlockSpec(memory_space=pltpu.SMEM)]
        + [pl.BlockSpec(memory_space=pltpu.VMEM)] * 8,
        out_specs=pl.BlockSpec(memory_space=pltpu.VMEM),
        scratch_shapes=[
            pltpu.VMEM((ROWS, HD), jnp.bfloat16),
            pltpu.VMEM((ROWS, HD), jnp.bfloat16),
            pltpu.VMEM((ROWS, HD), jnp.float32),
        ],
        compiler_params=pltpu.CompilerParams(vmem_limit_bytes=VMEM_LIMIT),
        name="attn_cache",
    )(info, keys, values, lse, delta, dq, q_raw, d_attn, gain)


COLS = HEADS * HD
SIDE = HD // 2
CHIPS = 8
FEAT = D // 16


def project_kernel(idx_ref, gq_ref, gkv_ref, pq_ref, pkv_ref, wq_ref, wkv_ref, wr_ref, out_ref):
    total = contract_last(gq_ref[...], wq_ref[...])
    total += contract_last(gkv_ref[...], wkv_ref[...])
    total += contract_last(pq_ref[...], wr_ref[0, :, :COLS])
    total += contract_last(pkv_ref[...], wr_ref[0, :, COLS:])
    out_ref[0] = total.astype(jnp.bfloat16)


def project(idx, grad_q, grad_kv, pair_q, pair_kv, w_query, w_kv, w_pair):
    def whole(j, idx):
        return (0, 0)

    def own(j, idx):
        return (2 * j + idx[1], 0)

    return pl.pallas_call(
        project_kernel,
        out_shape=jax.ShapeDtypeStruct((CHIPS, TOK, FEAT), jnp.bfloat16),
        grid_spec=pltpu.PrefetchScalarGridSpec(
            num_scalar_prefetch=1,
            grid=(CHIPS,),
            in_specs=[
                pl.BlockSpec((TOK, COLS), whole),
                pl.BlockSpec((TOK, HD), whole),
                pl.BlockSpec((TOK, COLS), whole),
                pl.BlockSpec((TOK, HD), whole),
                pl.BlockSpec((FEAT, COLS), own),
                pl.BlockSpec((FEAT, HD), own),
                pl.BlockSpec((1, FEAT, COLS + HD), lambda j, idx: (j, 0, 0)),
            ],
            out_specs=pl.BlockSpec((1, TOK, FEAT), lambda j, idx: (j, 0, 0)),
        ),
        compiler_params=pltpu.CompilerParams(vmem_limit_bytes=VMEM_LIMIT),
        name="project",
    )(idx, grad_q, grad_kv, pair_q, pair_kv, w_query, w_kv, w_pair)


def shift(block, axis, by):
    count = lax.axis_size(axis)
    return lax.ppermute(block, axis, [(i, (i + by) % count) for i in range(count)])


def swap(block, axis):
    return shift(block, axis, 1)


def on_device(
    residual_in,
    dh_rest,
    w_query,
    w_key,
    w_value,
    q_raw,
    k_raw,
    v_win,
    cache_k,
    cache_v,
    d_attn,
    s_qk,
    cache_live,
):
    z = lax.axis_index("z")
    xh = lax.axis_index("xh")
    chip = lax.axis_index("xl") * 4 + lax.axis_index("y")
    core = lax.axis_index("c")
    ctx = z * 2 + xh
    idx = jnp.stack([chip, core]).astype(jnp.int32)
    gain = s_qk.reshape(1, HD)

    here = pack_rows(idx, cache_k, cache_v, k_raw, v_win, gain)
    there = swap(here, "xh")
    up = shift(here, "z", -1)
    down = shift(here, "z", 1)
    up_there = shift(there, "z", -1)
    down_there = shift(there, "z", 1)
    far_a = shift(up[:CUT], "z", -1)
    far_b = shift(down[CUT:], "z", 1)
    far_there_a = shift(up_there[:CUT], "z", -1)
    far_there_b = shift(down_there[CUT:], "z", 1)
    mine = [here, there, up, down, up_there, down_there, far_a, far_b, far_there_a, far_there_b]
    other = [swap(piece, "c") for piece in mine]

    def source(dz, dx):
        return ((z + dz) % 4) * 2 + (xh + dx) % 2

    hops = [(0, 0), (0, 1), (1, 0), (3, 0), (1, 1), (3, 1), (2, 0), (2, 1)]
    info = jnp.stack(
        [source(dz, dx) for dz, dx in hops] + [CACHE - cache_live[0], ctx, core]
    ).astype(jnp.int32)

    w_kv = jnp.concatenate([w_key, w_value], 1)
    w_blocks = jnp.concatenate(
        [w_query.reshape(CHIPS, 2, FEAT, COLS), w_kv.reshape(CHIPS, 2, FEAT, HD)], 3
    )
    w_pair = swap(
        lax.dynamic_index_in_dim(w_blocks, 1 - core, 1, keepdims=False), "c"
    )

    keys, values, lse, delta, dq, dkv = stats_call(info, mine + other, q_raw, d_attn, gain)
    dkv = dkv.reshape(CTX, TOK, 2 * HD)
    dkv_own = lax.dynamic_index_in_dim(dkv, ctx, 0, keepdims=False)
    arrived = []
    for dz, dx in hops[1:]:
        part = lax.dynamic_index_in_dim(dkv, source(dz, dx), 0, keepdims=False)
        route = []
        for a in range(4):
            for b in range(2):
                route.append((a * 2 + b, ((a + dz) % 4) * 2 + (b + dx) % 2))
        arrived.append(lax.ppermute(part, CTX_AXES, route))
    grad_q = cache_call(info, keys, values, lse, delta, dq, q_raw, d_attn, gain)
    for part in arrived:
        dkv_own = dkv_own + part
    dkv_own = dkv_own + swap(dkv_own, "c")
    key_raw = lax.dynamic_slice_in_dim(k_raw, chip * HD, HD, 1).astype(jnp.float32)
    grad_k = unit_back(key_raw, s_qk, dkv_own[:, :HD]).astype(jnp.bfloat16)
    grad_v = dkv_own[:, HD:].astype(jnp.bfloat16)
    low = jnp.concatenate([grad_k[:, :SIDE], grad_v[:, :SIDE]], 1)
    high = jnp.concatenate([grad_k[:, SIDE:], grad_v[:, SIDE:]], 1)
    own_kv = jnp.where(core == 0, low, high)
    pair_kv = jnp.where(core == 0, high, low)
    pair_q = swap(grad_q, "c")

    partial = project(idx, grad_q, own_kv, pair_q, pair_kv, w_query, w_kv, w_pair)
    pieces = lax.all_to_all(partial, CHIP_AXES, 0, 0)
    grad_total = jnp.sum(pieces.astype(jnp.float32), axis=0) + dh_rest.astype(jnp.float32)
    resid = residual_in.astype(jnp.float32)
    sums = jnp.stack([jnp.sum(resid * resid, axis=1), jnp.sum(grad_total * resid, axis=1)])
    everyone = lax.all_to_all(
        jnp.broadcast_to(sums[None], (16, 2, TOK)), TP_AXES, 0, 0
    )
    square_sum, inner_sum = jnp.sum(everyone, axis=0)
    mean_sq = square_sum / D
    factor = lax.rsqrt(mean_sq + EPS) / math.sqrt(D)
    correction = inner_sum / (D * (mean_sq + EPS))
    return factor[:, None] * (grad_total - resid * correction[:, None])


def solution(mesh):
    fine = Mesh(mesh.devices.reshape(4, 2, 2, 4, 2), ("z", "xh", "xl", "y", "c"))
    both = P(CTX_AXES, TP_AXES)
    cols = P(None, TP_AXES)
    rows = P(CTX_AXES, None)
    return jax.shard_map(
        on_device,
        mesh=fine,
        in_specs=(both, both, cols, cols, cols, both, rows, rows, rows, rows, both, P(), P()),
        out_specs=both,
        check_vma=False,
    )
```

```python
import functools
import math

import jax
import jax.numpy as jnp
from jax import lax
from jax.experimental import pallas as pl
from jax.experimental.pallas import tpu as pltpu
from jax.sharding import Mesh
from jax.sharding import PartitionSpec as P

D = 8192
KVH = 8
HD = 128
CACHE = 8192
TOKENS = 1024
CTX = 8
TOK = TOKENS // CTX
HEADS = 4
ROWS = 2 * HEADS * TOK
COLS = HEADS * HD
SIDE = HD // 2
CHIPS = 8
FEAT = D // 16
HALF_CACHE = CACHE // CTX // 2
HALF_WIN = TOK // 2
HALF = HALF_CACHE + HALF_WIN
CUT = HALF // 2
KB = 512
CHUNK = 512
CHUNKS = ROWS // CHUNK
EPS = 1e-06
SCALE = math.sqrt(HD)
EXP_SCALE = SCALE * math.log2(math.e)
NEG = -1e30
VMEM_LIMIT = 28 * 1024 * 1024
TP_AXES = ("xl", "y", "c")
CTX_AXES = ("z", "xh")
CHIP_AXES = ("xl", "y")


def contract_last(left, right):
    return lax.dot_general(
        left, right, (((1,), (1,)), ((), ())), preferred_element_type=jnp.float32
    )


def contract_first(left, right):
    return lax.dot_general(
        left, right, (((0,), (0,)), ((), ())), preferred_element_type=jnp.float32
    )


def unit_rows(values, qk_gain):
    width = values.shape[-1]
    mean_sq = jnp.mean(values * values, axis=-1, keepdims=True)
    return values * (lax.rsqrt(mean_sq + EPS) / math.sqrt(width)) * qk_gain


def unit_back(values, qk_gain, grad):
    width = values.shape[-1]
    mean_sq = jnp.mean(values * values, axis=-1, keepdims=True)
    factor = lax.rsqrt(mean_sq + EPS) / math.sqrt(width)
    weighted = qk_gain * grad
    inner = jnp.sum(weighted * values, axis=-1, keepdims=True)
    return factor * (weighted - values * inner / (width * (mean_sq + EPS)))


def head_cols(h):
    return slice(h * HD, (h + 1) * HD)


def head_rows(h):
    return slice(h * TOK, (h + 1) * TOK)


def pack_kernel(idx_ref, ck_ref, cv_ref, kr_ref, vw_ref, gain_ref, out_ref):
    gain = gain_ref[...]
    out_ref[:HALF_CACHE, :HD] = unit_rows(ck_ref[...].astype(jnp.float32), gain).astype(
        jnp.bfloat16
    )
    out_ref[:HALF_CACHE, HD:] = cv_ref[...]
    out_ref[HALF_CACHE:, :HD] = unit_rows(kr_ref[...].astype(jnp.float32), gain).astype(
        jnp.bfloat16
    )
    out_ref[HALF_CACHE:, HD:] = vw_ref[...]


def pack_rows(idx, cache_k, cache_v, k_raw, v_win, gain):
    def at(i, idx):
        return (idx[CORE], idx[CHIP])

    return pl.pallas_call(
        pack_kernel,
        out_shape=jax.ShapeDtypeStruct((HALF, 2 * HD), jnp.bfloat16),
        grid_spec=pltpu.PrefetchScalarGridSpec(
            num_scalar_prefetch=1,
            grid=(1,),
            in_specs=[
                pl.BlockSpec((HALF_CACHE, HD), at),
                pl.BlockSpec((HALF_CACHE, HD), at),
                pl.BlockSpec((HALF_WIN, HD), at),
                pl.BlockSpec((HALF_WIN, HD), at),
                pl.BlockSpec((1, HD), lambda i, idx: (0, 0)),
            ],
            out_specs=pl.BlockSpec((HALF, 2 * HD), lambda i, idx: (0, 0)),
        ),
        compiler_params=pltpu.CompilerParams(vmem_limit_bytes=8 * 1024 * 1024),
        name="pack_rows",
    )(idx, cache_k, cache_v, k_raw, v_win, gain)


def cost(flops, exps, moved):
    return pl.CostEstimate(
        flops=int(flops), transcendentals=int(exps), bytes_accessed=int(moved)
    )


def block_cost(blocks, dots):
    return cost(
        blocks * dots * 2 * ROWS * KB * HD, blocks * ROWS * KB, blocks * 4 * KB * HD + 2 ** 21
    )


HOPS = ((0, 0), (0, 1), (1, 0), (3, 0), (1, 1), (3, 1), (2, 0), (2, 1))
Z, XH, CHIP, CORE, FLOOR = range(5)


def source(info_ref, dz, dx):
    return lax.bitwise_and(info_ref[Z] + dz, 3) * 2 + lax.bitwise_and(info_ref[XH] + dx, 1)


def source_at(info_ref, n):
    dz = jnp.where(n >= 6, 2, jnp.where(n < 2, 0, jnp.where(lax.bitwise_and(n, 1) == 0, 1, 3)))
    dx = jnp.where(n >= 6, n - 6, jnp.where(n < 2, n, jnp.where(n >= 4, 1, 0)))
    return source(info_ref, dz, dx)


def cache_mask(info_ref, start):
    return start + lax.broadcasted_iota(jnp.int32, (CHUNK, KB), 1) >= info_ref[FLOOR]


def window_mask(info_ref):
    local = lax.broadcasted_iota(jnp.int32, (CHUNK, KB), 1)
    key = (
        lax.shift_right_logical(local, 6) * TOK
        + info_ref[CORE] * HALF_WIN
        + lax.bitwise_and(local, jnp.int32(HALF_WIN - 1))
    )
    token = source(info_ref, 0, 0) * TOK + lax.bitwise_and(
        lax.broadcasted_iota(jnp.int32, (CHUNK, KB), 0), jnp.int32(TOK - 1)
    )
    return key <= token


def chunk(r):
    return pl.ds(pl.multiple_of(r * CHUNK, CHUNK), CHUNK)


def keys_at(n):
    return pl.ds(pl.multiple_of(n * KB, KB), KB)


def place_cache(pieces, k_s, v_s, at=0):
    for n, group in enumerate(pieces):
        row = (at + n) * KB
        for piece in group:
            rows = min(piece.shape[0], (at + n + 1) * KB - row)
            k_s[row : row + rows, :] = piece[:rows, :HD]
            v_s[row : row + rows, :] = piece[:rows, HD:]
            row += rows


def stat_block(scores, dprobs, mask, rows, m_s, l_s, w_s):
    if mask is not None:
        scores = jnp.where(mask, scores, NEG)
    old = m_s[rows, :]
    top = old
    for g in range(KB // HD):
        top = jnp.maximum(top, scores[:, head_cols(g)])
    keep = jnp.exp2((old - top) * EXP_SCALE)
    total = l_s[rows, :] * keep
    weighted = w_s[rows, :] * keep
    for g in range(KB // HD):
        e = jnp.exp2((scores[:, head_cols(g)] - top) * EXP_SCALE)
        if mask is not None:
            e = jnp.where(mask[:, head_cols(g)], e, 0.0)
        total = total + e
        weighted = weighted + e * dprobs[:, head_cols(g)]
    m_s[rows, :] = top
    l_s[rows, :] = total
    w_s[rows, :] = weighted


def cache_loop(info_ref, first, count, core, body):
    @pl.loop(0, count * CHUNKS)
    def _(i):
        n = i // CHUNKS
        r = lax.rem(i, CHUNKS)
        start = source_at(info_ref, first + n) * (2 * KB) + core * KB

        @pl.when((start + KB > info_ref[FLOOR]) & (start < info_ref[FLOOR]))
        def _():
            body(n, r, start, True)

        @pl.when(start >= info_ref[FLOOR])
        def _():
            body(n, r, start, False)


def stats_kernel(first, groups, last, info_ref, *refs):
    refs = list(refs)
    flat = [refs.pop(0) for _ in range(sum(groups))]
    pieces = []
    for size in groups:
        pieces.append([flat.pop(0) for _ in range(size)])
    core = info_ref[CORE]
    if first == 0:
        q_ref, do_ref, pair_q_ref, pair_do_ref, gain_ref = refs[:5]
        q_s, do_s, m_s, l_s, w_s = refs[5:10]
        scratch = refs[10:]
        gain = gain_ref[...]
        for side, (raw_ref, grad_ref) in enumerate(((q_ref, do_ref), (pair_q_ref, pair_do_ref))):
            for h in range(HEADS):
                rows = slice((side * HEADS + h) * TOK, (side * HEADS + h + 1) * TOK)
                raw = raw_ref[:, head_cols(h)].astype(jnp.float32)
                q_s[rows, :] = unit_rows(raw, gain).astype(jnp.bfloat16)
                do_s[rows, :] = grad_ref[:, head_cols(h)]
        m_s[...] = jnp.full((ROWS, HD), NEG, jnp.float32)
        l_s[...] = jnp.zeros((ROWS, HD), jnp.float32)
        w_s[...] = jnp.zeros((ROWS, HD), jnp.float32)
    else:
        wins = []
        if last:
            wins = [refs.pop(0) for _ in range(CTX - 1)]
        q_s, do_s, m_in, l_in, w_in = refs[:5]
        if last:
            stat_ref, wk_ref, wv_ref = refs[5:8]
            m_s, l_s, w_s = refs[8:11]
            scratch = refs[11:]
        else:
            m_s, l_s, w_s = refs[5:8]
            scratch = refs[8:]
        m_s[...] = m_in[...]
        l_s[...] = l_in[...]
        w_s[...] = w_in[...]
    k_s, v_s = scratch
    place_cache(pieces, k_s, v_s)

    def body(n, r, start, masked):
        scores = contract_last(q_s[chunk(r), :], k_s[keys_at(n), :])
        dprobs = contract_last(do_s[chunk(r), :], v_s[keys_at(n), :])
        mask = cache_mask(info_ref, start) if masked else None
        stat_block(scores, dprobs, mask, chunk(r), m_s, l_s, w_s)

    cache_loop(info_ref, first, len(groups), core, body)
    if last:
        for n, piece in enumerate(wins + [pieces[-1][-1]]):
            at = pl.multiple_of(source(info_ref, *HOPS[n]) * HALF_WIN, HALF_WIN)
            low = piece.shape[0] - HALF_WIN
            wk_ref[pl.ds(at, HALF_WIN), :] = piece[low:, :HD]
            wv_ref[pl.ds(at, HALF_WIN), :] = piece[low:, HD:]

        @pl.loop(0, CHUNKS)
        def _(r):
            scores = contract_last(q_s[chunk(r), :], wk_ref[...])
            dprobs = contract_last(do_s[chunk(r), :], wv_ref[...])
            stat_block(scores, dprobs, window_mask(info_ref), chunk(r), m_s, l_s, w_s)

        top = jnp.max(m_s[...], axis=1, keepdims=True)
        fix = jnp.exp2((m_s[...] - top) * EXP_SCALE)
        total = jnp.sum(l_s[...] * fix, axis=1, keepdims=True)
        weighted = jnp.sum(w_s[...] * fix, axis=1, keepdims=True)
        lane = lax.broadcasted_iota(jnp.int32, (ROWS, HD), 1)
        stat_ref[...] = jnp.where(lane == 0, top, jnp.where(lane == 1, total, weighted))


SHAPE = jax.ShapeDtypeStruct
STATE = [SHAPE((ROWS, HD), jnp.float32)] * 3
VM = pl.BlockSpec(memory_space=pltpu.VMEM)
SM = pl.BlockSpec(memory_space=pltpu.SMEM)


def stats_call(first, info, groups, rest, last=False):
    pieces = [piece for group in groups for piece in group]
    if first == 0:
        out = [SHAPE((ROWS, HD), jnp.bfloat16)] * 2 + STATE
    elif last:
        out = [SHAPE((ROWS, HD), jnp.float32)] + [SHAPE((KB, HD), jnp.bfloat16)] * 2
    else:
        out = STATE
    keys = len(groups) * KB
    scratch = [pltpu.VMEM((keys, HD), jnp.bfloat16)] * 2
    if last:
        scratch = [pltpu.VMEM((ROWS, HD), jnp.float32)] * 3 + scratch
    return pl.pallas_call(
        functools.partial(stats_kernel, first, [len(group) for group in groups], last),
        out_shape=out,
        in_specs=[SM] + [VM] * (len(pieces) + len(rest)),
        out_specs=[VM] * len(out),
        scratch_shapes=scratch,
        compiler_params=pltpu.CompilerParams(vmem_limit_bytes=VMEM_LIMIT),
        cost_estimate=block_cost(len(groups) + (1 if last else 0), 2),
        name="stats_" + str(first),
    )(info, *pieces, *rest)


def grad_block(scores, dprobs, mask, lse, delta):
    probs = []
    dscores = []
    for g in range(KB // HD):
        p = jnp.exp2(scores[:, head_cols(g)] * EXP_SCALE - lse)
        if mask is not None:
            p = jnp.where(mask[:, head_cols(g)], p, 0.0)
        probs.append(p.astype(jnp.bfloat16))
        dscores.append((p * (dprobs[:, head_cols(g)] - delta)).astype(jnp.bfloat16))
    return jnp.concatenate(probs, 1), jnp.concatenate(dscores, 1)


def window_kernel(
    info_ref, mine_ref, pair_ref, q_s, do_s, wk_ref, wv_ref, lse_ref, delta_ref, dq_ref, *rest
):
    parts, dkv_ref = rest[:4], rest[4]
    mine = mine_ref[...]
    half = ROWS // 2
    pair = jnp.concatenate([pair_ref[half:, :], pair_ref[:half, :]], 0)
    top = jnp.maximum(mine[:, 0:1], pair[:, 0:1])
    fix = jnp.exp2((mine[:, 0:1] - top) * EXP_SCALE)
    pair_fix = jnp.exp2((pair[:, 0:1] - top) * EXP_SCALE)
    total = mine[:, 1:2] * fix + pair[:, 1:2] * pair_fix
    weighted = mine[:, 2:3] * fix + pair[:, 2:3] * pair_fix
    lse_ref[...] = jnp.broadcast_to(top * EXP_SCALE + jnp.log2(total), (ROWS, HD))
    delta_ref[...] = jnp.broadcast_to(weighted / total, (ROWS, HD))
    dkv_ref[...] = jnp.zeros((KB, 2 * HD), jnp.float32)

    @pl.loop(0, CHUNKS)
    def _(r):
        rows = chunk(r)
        query = q_s[rows, :]
        dout = do_s[rows, :]
        scores = contract_last(query, wk_ref[...])
        dprobs = contract_last(dout, wv_ref[...])
        probs, dscores = grad_block(
            scores, dprobs, window_mask(info_ref), lse_ref[rows, :], delta_ref[rows, :]
        )
        dq_ref[rows, :] = jnp.dot(dscores, wk_ref[...], preferred_element_type=jnp.float32)
        dkv_ref[:, :HD] += contract_first(dscores, query)
        dkv_ref[:, HD:] += contract_first(probs, dout)

    for dz in range(4):
        at = pl.multiple_of(lax.bitwise_and(info_ref[Z] + dz, 3) * TOK, TOK)
        parts[dz][...] = dkv_ref[pl.ds(at, TOK), :]


def window_call(info, mine, pair, query, dout, win_k, win_v):
    out = STATE + [SHAPE((TOK, 2 * HD), jnp.float32)] * 4
    return pl.pallas_call(
        window_kernel,
        out_shape=out,
        in_specs=[SM] + [VM] * 6,
        out_specs=[VM] * 7,
        scratch_shapes=[pltpu.VMEM((KB, 2 * HD), jnp.float32)],
        compiler_params=pltpu.CompilerParams(vmem_limit_bytes=VMEM_LIMIT),
        cost_estimate=block_cost(1, 5),
        name="window_grads",
    )(info, mine, pair, query, dout, win_k, win_v)


def cache_kernel(first, groups, info_ref, *refs):
    refs = list(refs)
    pieces = []
    for size in groups:
        pieces.append([refs.pop(0) for _ in range(size)])
    q_s, do_s, lse_ref, delta_ref, dq_in, dq_ref, k_s, v_s = refs
    place_cache(pieces, k_s, v_s)
    dq_ref[...] = dq_in[...]

    def body(n, r, start, masked):
        rows = chunk(r)
        keys = k_s[keys_at(n), :]
        scores = contract_last(q_s[rows, :], keys)
        dprobs = contract_last(do_s[rows, :], v_s[keys_at(n), :])
        mask = cache_mask(info_ref, start) if masked else None
        _, dscores = grad_block(scores, dprobs, mask, lse_ref[rows, :], delta_ref[rows, :])
        dq_ref[rows, :] += jnp.dot(dscores, keys, preferred_element_type=jnp.float32)

    cache_loop(info_ref, first, len(groups), info_ref[CORE], body)


def cache_call(first, info, groups, query, dout, lse, delta, dq):
    pieces = [piece for group in groups for piece in group]
    return pl.pallas_call(
        functools.partial(cache_kernel, first, [len(group) for group in groups]),
        out_shape=STATE[0],
        in_specs=[SM] + [VM] * (len(pieces) + 5),
        out_specs=VM,
        scratch_shapes=[pltpu.VMEM((len(groups) * KB, HD), jnp.bfloat16)] * 2,
        compiler_params=pltpu.CompilerParams(vmem_limit_bytes=VMEM_LIMIT),
        cost_estimate=block_cost(len(groups), 3),
        name="cache_grads_" + str(first),
    )(info, *pieces, query, dout, lse, delta, dq)


SMALL = pltpu.CompilerParams(vmem_limit_bytes=8 * 1024 * 1024)


def sum_kernel(info_ref, a_ref, b_ref, c_ref, d_ref, keep_ref, send_ref):
    total = (a_ref[...] + b_ref[...]) + (c_ref[...] + d_ref[...])
    first = info_ref[XH] == 0
    keep_ref[...] = jnp.where(first, total[:HALF_WIN, :], total[HALF_WIN:, :])
    send_ref[...] = jnp.where(first, total[HALF_WIN:, :], total[:HALF_WIN, :])


def sum_parts(info, parts):
    return pl.pallas_call(
        sum_kernel,
        out_shape=[SHAPE((HALF_WIN, 2 * HD), jnp.float32)] * 2,
        in_specs=[SM] + [VM] * 4,
        out_specs=[VM] * 2,
        compiler_params=SMALL,
        name="sum_parts",
    )(info, *parts)


def own_kv_kernel(idx_ref, keep_ref, other_ref, raw_ref, gain_ref, out_ref):
    total = keep_ref[...] + other_ref[...]
    raw = raw_ref[...].astype(jnp.float32)
    out_ref[:, :HD] = unit_back(raw, gain_ref[...], total[:, :HD] * SCALE).astype(jnp.bfloat16)
    out_ref[:, HD:] = total[:, HD:].astype(jnp.bfloat16)


def own_kv(idx, keep, other, k_raw, gain):
    def whole(i, idx):
        return (0, 0)

    return pl.pallas_call(
        own_kv_kernel,
        out_shape=SHAPE((HALF_WIN, 2 * HD), jnp.bfloat16),
        grid_spec=pltpu.PrefetchScalarGridSpec(
            num_scalar_prefetch=1,
            grid=(1,),
            in_specs=[
                pl.BlockSpec((HALF_WIN, 2 * HD), whole),
                pl.BlockSpec((HALF_WIN, 2 * HD), whole),
                pl.BlockSpec((HALF_WIN, HD), lambda i, idx: (idx[CORE], idx[CHIP])),
                pl.BlockSpec((1, HD), whole),
            ],
            out_specs=pl.BlockSpec((HALF_WIN, 2 * HD), whole),
        ),
        compiler_params=SMALL,
        name="own_kv",
    )(idx, keep, other, k_raw, gain)


def project_kernel(
    idx_ref,
    dq_ref,
    pair_dq_ref,
    q_ref,
    pair_q_ref,
    gain_ref,
    kv_ref,
    pair_kv_ref,
    wq_ref,
    wk_ref,
    wv_ref,
    pair_wq_ref,
    pair_wk_ref,
    pair_wv_ref,
    out_ref,
    g_s,
):
    core = idx_ref[CORE]
    gain = gain_ref[...]
    for h in range(HEADS):
        rows = head_rows(h)
        low = slice(ROWS // 2 + h * TOK, ROWS // 2 + (h + 1) * TOK)
        for side, raw_ref, grad in (
            (0, q_ref, dq_ref[rows, :] + pair_dq_ref[low, :]),
            (1, pair_q_ref, dq_ref[low, :] + pair_dq_ref[rows, :]),
        ):
            raw = raw_ref[:, head_cols(h)].astype(jnp.float32)
            at = side * COLS + h * HD
            g_s[at : at + HD, :] = unit_back(raw, gain, grad * SCALE).T.astype(jnp.bfloat16)
    here = kv_ref[...].astype(jnp.float32)
    there = pair_kv_ref[...].astype(jnp.float32)
    top = jnp.where(core == 0, here, there)
    bottom = jnp.where(core == 0, there, here)
    kv = jnp.concatenate([top, bottom], 0)
    for n in range(2):
        both = kv[:, n * HD : (n + 1) * HD].T.astype(jnp.bfloat16)
        first = jnp.where(core == 0, both[:SIDE, :], both[SIDE:, :])
        second = jnp.where(core == 0, both[SIDE:, :], both[:SIDE, :])
        g_s[2 * COLS + n * SIDE : 2 * COLS + (n + 1) * SIDE, :] = first
        g_s[2 * COLS + (2 + n) * SIDE : 2 * COLS + (3 + n) * SIDE, :] = second

    @pl.loop(0, CHIPS)
    def _(j):
        rows = pl.ds(pl.multiple_of((2 * j + core) * FEAT, FEAT), FEAT)
        total = jnp.dot(wq_ref[rows, :], g_s[:COLS, :], preferred_element_type=jnp.float32)
        total += jnp.dot(
            pair_wq_ref[rows, :], g_s[COLS : 2 * COLS, :], preferred_element_type=jnp.float32
        )
        narrow = jnp.concatenate(
            [wk_ref[:, rows], wv_ref[:, rows], pair_wk_ref[:, rows], pair_wv_ref[:, rows]], 0
        )
        total += contract_first(narrow, g_s[2 * COLS :, :])
        out_ref[j] = total.astype(jnp.bfloat16)


def project(idx, dq, pair_dq, q_raw, pair_q, gain, kv, pair_kv, weights, pair_weights):
    return pl.pallas_call(
        project_kernel,
        out_shape=jax.ShapeDtypeStruct((CHIPS, FEAT, TOK), jnp.bfloat16),
        in_specs=[SM] + [VM] * 13,
        out_specs=VM,
        scratch_shapes=[pltpu.VMEM((2 * COLS + 2 * HD, TOK), jnp.bfloat16)],
        compiler_params=pltpu.CompilerParams(vmem_limit_bytes=VMEM_LIMIT),
        cost_estimate=cost(2 * TOK * D // 2 * 1280, 0, 3e6),
        name="project",
    )(idx, dq, pair_dq, q_raw, pair_q, gain, kv, pair_kv, *weights, *pair_weights)


def shift(block, axis, by):
    count = lax.axis_size(axis)
    return lax.ppermute(block, axis, [(i, (i + by) % count) for i in range(count)])


def swap(block, axis):
    return shift(block, axis, 1)


def on_device(
    residual_in,
    dh_rest,
    w_query,
    w_key,
    w_value,
    q_raw,
    k_raw,
    v_win,
    cache_k,
    cache_v,
    d_attn,
    s_qk,
    cache_live,
):
    info = jnp.stack(
        [
            lax.axis_index("z"),
            lax.axis_index("xh"),
            lax.axis_index("xl") * 4 + lax.axis_index("y"),
            lax.axis_index("c"),
            CACHE - cache_live[0],
        ]
    ).astype(jnp.int32)
    gain = s_qk.reshape(1, HD)

    here = pack_rows(info, cache_k, cache_v, k_raw, v_win, gain)
    there = swap(here, "xh")
    up = shift(here, "z", -1)
    down = shift(here, "z", 1)
    pair_q = swap(q_raw, "c")
    pair_do = swap(d_attn, "c")
    up_there = shift(there, "z", -1)
    down_there = shift(there, "z", 1)
    far = [shift(up[:CUT], "z", -1), shift(down[CUT:], "z", 1)]
    groups = [[here], [there], [up], [down]]
    weights = (w_query, w_key.T, w_value.T)
    pair_weights = [swap(w, "c") for w in weights]

    query, dout, *state = stats_call(
        0, info, groups[:4], [q_raw, d_attn, pair_q, pair_do, gain]
    )
    query, dout, state, up_there, down_there = lax.optimization_barrier(
        (query, dout, state, up_there, down_there)
    )
    far_there = [shift(up_there[:CUT], "z", -1), shift(down_there[CUT:], "z", 1)]
    groups += [[up_there], [down_there], far, far_there]
    state = stats_call(4, info, groups[4:7], [query, dout, *state])
    wins = [group[-1] for group in groups[:-1]]
    stat, win_k, win_v = stats_call(
        7, info, groups[7:], wins + [query, dout, *state], last=True
    )
    lse, delta, dq, *parts = window_call(
        info, stat, swap(stat, "c"), query, dout, win_k, win_v
    )
    parts = [parts[0]] + [shift(parts[dz], "z", dz) for dz in (1, 3, 2)]
    dq = cache_call(0, info, groups[:4], query, dout, lse, delta, dq)
    parts, dq = lax.optimization_barrier((parts, dq))
    keep, send = sum_parts(info, parts)
    other = swap(send, "xh")
    dq = cache_call(4, info, groups[4:], query, dout, lse, delta, dq)
    other, dq = lax.optimization_barrier((other, dq))
    pair_dq = swap(dq, "c")
    kv = own_kv(info, keep, other, k_raw, gain)
    pair_kv = swap(kv, "c")
    partial = project(
        info, dq, pair_dq, q_raw, pair_q, gain, kv, pair_kv, weights, pair_weights
    )
    pieces = lax.all_to_all(partial, CHIP_AXES, 0, 0)
    grad_total = jnp.sum(pieces.astype(jnp.float32), axis=0).T + dh_rest.astype(jnp.float32)
    resid = residual_in.astype(jnp.float32)
    sums = jnp.stack([jnp.sum(resid * resid, axis=1), jnp.sum(grad_total * resid, axis=1)])
    everyone = lax.all_to_all(
        jnp.broadcast_to(sums[None], (16, 2, TOK)), TP_AXES, 0, 0
    )
    square_sum, inner_sum = jnp.sum(everyone, axis=0)
    mean_sq = square_sum / D
    factor = lax.rsqrt(mean_sq + EPS) / math.sqrt(D)
    correction = inner_sum / (D * (mean_sq + EPS))
    return factor[:, None] * (grad_total - resid * correction[:, None])


def solution(mesh):
    fine = Mesh(mesh.devices.reshape(4, 2, 2, 4, 2), ("z", "xh", "xl", "y", "c"))
    both = P(CTX_AXES, TP_AXES)
    cols = P(None, TP_AXES)
    rows = P(CTX_AXES, None)
    return jax.shard_map(
        on_device,
        mesh=fine,
        in_specs=(both, both, cols, cols, cols, both, rows, rows, rows, rows, both, P(), P()),
        out_specs=both,
        check_vma=False,
    )
```

```python
import functools
import math

import jax
import jax.numpy as jnp
from jax import lax
from jax.experimental import pallas as pl
from jax.experimental.pallas import tpu as pltpu
from jax.sharding import Mesh
from jax.sharding import PartitionSpec as P

D = 8192
KVH = 8
HD = 128
CACHE = 8192
TOKENS = 1024
CTX = 8
TOK = TOKENS // CTX
HEADS = 4
ROWS = 2 * HEADS * TOK
COLS = HEADS * HD
SIDE = HD // 2
CHIPS = 8
FEAT = D // 16
HALF_CACHE = CACHE // CTX // 2
HALF_WIN = TOK // 2
HALF = HALF_CACHE + HALF_WIN
CUT = HALF // 2
KB = 512
CHUNK = 512
CHUNKS = ROWS // CHUNK
EPS = 1e-06
SCALE = math.sqrt(HD)
EXP_SCALE = SCALE * math.log2(math.e)
NEG = -1e30
VMEM_LIMIT = 24 * 1024 * 1024
TP_AXES = ("xl", "y", "c")
CTX_AXES = ("z", "xh")
CHIP_AXES = ("xl", "y")


HOPS = ((0, 0), (0, 1), (1, 0), (3, 0), (1, 1), (3, 1), (2, 0), (2, 1))
Z, XH, CHIP, CORE, FLOOR = range(5)
SHAPE = jax.ShapeDtypeStruct
STATE = [SHAPE((ROWS, HD), jnp.float32)] * 3
VM = pl.BlockSpec(memory_space=pltpu.VMEM)
SM = pl.BlockSpec(memory_space=pltpu.SMEM)
HB = pl.BlockSpec(memory_space=pltpu.HBM)
SMALL = pltpu.CompilerParams(vmem_limit_bytes=8 * 1024 * 1024)


def contract_last(left, right):
    return lax.dot_general(
        left, right, (((1,), (1,)), ((), ())), preferred_element_type=jnp.float32
    )


def contract_first(left, right):
    return lax.dot_general(
        left, right, (((0,), (0,)), ((), ())), preferred_element_type=jnp.float32
    )


def unit_rows(values, qk_gain):
    width = values.shape[-1]
    mean_sq = jnp.mean(values * values, axis=-1, keepdims=True)
    return values * (lax.rsqrt(mean_sq + EPS) / math.sqrt(width)) * qk_gain


def unit_back(values, qk_gain, grad):
    width = values.shape[-1]
    mean_sq = jnp.mean(values * values, axis=-1, keepdims=True)
    factor = lax.rsqrt(mean_sq + EPS) / math.sqrt(width)
    weighted = qk_gain * grad
    inner = jnp.sum(weighted * values, axis=-1, keepdims=True)
    return factor * (weighted - values * inner / (width * (mean_sq + EPS)))


def head_cols(h):
    return slice(h * HD, (h + 1) * HD)


def head_rows(h):
    return slice(h * TOK, (h + 1) * TOK)


def pack_kernel(
    info_ref,
    ck_ref,
    cv_ref,
    kr_ref,
    vw_ref,
    resid_ref,
    dh_ref,
    gain_ref,
    out_ref,
    resid_out,
    dh_out,
    ck_s,
    kr_s,
    resid_s,
    dh_s,
    sems,
):
    cols = pl.ds(pl.multiple_of(info_ref[CHIP] * HD, HD), HD)
    cache = pl.ds(pl.multiple_of(info_ref[CORE] * HALF_CACHE, HALF_CACHE), HALF_CACHE)
    win = pl.ds(pl.multiple_of(info_ref[CORE] * HALF_WIN, HALF_WIN), HALF_WIN)
    right = pl.ds(HD, HD)
    copies = [
        pltpu.make_async_copy(ck_ref.at[cache, cols], ck_s, sems.at[0]),
        pltpu.make_async_copy(kr_ref.at[win, cols], kr_s, sems.at[1]),
        pltpu.make_async_copy(
            cv_ref.at[cache, cols], out_ref.at[pl.ds(0, HALF_CACHE), right], sems.at[2]
        ),
        pltpu.make_async_copy(
            vw_ref.at[win, cols], out_ref.at[pl.ds(HALF_CACHE, HALF_WIN), right], sems.at[3]
        ),
        pltpu.make_async_copy(resid_ref, resid_s, sems.at[4]),
        pltpu.make_async_copy(dh_ref, dh_s, sems.at[5]),
    ]
    for copy in copies:
        copy.start()
    gain = gain_ref[...]
    copies[0].wait()
    out_ref[:HALF_CACHE, :HD] = unit_rows(ck_s[...].astype(jnp.float32), gain).astype(jnp.bfloat16)
    copies[1].wait()
    out_ref[HALF_CACHE:, :HD] = unit_rows(kr_s[...].astype(jnp.float32), gain).astype(jnp.bfloat16)
    copies[2].wait()
    copies[3].wait()
    copies[4].wait()
    resid_out[...] = resid_s[...].astype(jnp.float32).T.astype(jnp.bfloat16)
    copies[5].wait()
    dh_out[...] = dh_s[...].astype(jnp.float32).T.astype(jnp.bfloat16)


def pack_rows(info, cache_k, cache_v, k_raw, v_win, resid, dh, gain):
    return pl.pallas_call(
        pack_kernel,
        out_shape=[
            SHAPE((HALF, 2 * HD), jnp.bfloat16),
            SHAPE((FEAT, TOK), jnp.bfloat16),
            SHAPE((FEAT, TOK), jnp.bfloat16),
        ],
        in_specs=[SM] + [HB] * 6 + [VM],
        out_specs=[VM] * 3,
        scratch_shapes=[
            pltpu.VMEM((HALF_CACHE, HD), jnp.bfloat16),
            pltpu.VMEM((HALF_WIN, HD), jnp.bfloat16),
            pltpu.VMEM((TOK, FEAT), jnp.bfloat16),
            pltpu.VMEM((TOK, FEAT), jnp.bfloat16),
            pltpu.SemaphoreType.DMA((6,)),
        ],
        compiler_params=SMALL,
        name="pack_rows",
    )(info, cache_k, cache_v, k_raw, v_win, resid, dh, gain)


def cost(flops, exps, moved):
    return pl.CostEstimate(
        flops=int(flops), transcendentals=int(exps), bytes_accessed=int(moved)
    )


def block_cost(blocks, dots):
    return cost(
        blocks * dots * 2 * ROWS * KB * HD, blocks * ROWS * KB, blocks * 4 * KB * HD + 2 ** 21
    )


def source(info_ref, dz, dx):
    return lax.bitwise_and(info_ref[Z] + dz, 3) * 2 + lax.bitwise_and(info_ref[XH] + dx, 1)


def source_at(info_ref, n):
    dz = jnp.where(n >= 6, 2, jnp.where(n < 2, 0, jnp.where(lax.bitwise_and(n, 1) == 0, 1, 3)))
    dx = jnp.where(n >= 6, n - 6, jnp.where(n < 2, n, jnp.where(n >= 4, 1, 0)))
    return source(info_ref, dz, dx)


def cache_mask(info_ref, start):
    return start + lax.broadcasted_iota(jnp.int32, (CHUNK, KB), 1) >= info_ref[FLOOR]


def window_mask(info_ref):
    local = lax.broadcasted_iota(jnp.int32, (CHUNK, KB), 1)
    key = (
        lax.shift_right_logical(local, 6) * TOK
        + info_ref[CORE] * HALF_WIN
        + lax.bitwise_and(local, jnp.int32(HALF_WIN - 1))
    )
    token = source(info_ref, 0, 0) * TOK + lax.bitwise_and(
        lax.broadcasted_iota(jnp.int32, (CHUNK, KB), 0), jnp.int32(TOK - 1)
    )
    return key <= token


def chunk(r):
    return slice(r * CHUNK, (r + 1) * CHUNK)


def keys_at(n):
    return pl.ds(pl.multiple_of(n * KB, KB), KB)


def place_cache(pieces, k_s, v_s, at=0):
    for n, group in enumerate(pieces):
        row = (at + n) * KB
        for piece in group:
            rows = min(piece.shape[0], (at + n + 1) * KB - row)
            k_s[row : row + rows, :] = piece[:rows, :HD]
            v_s[row : row + rows, :] = piece[:rows, HD:]
            row += rows


def stat_block(scores, dprobs, mask, rows, m_s, l_s, w_s):
    if mask is not None:
        scores = jnp.where(mask, scores, NEG)
    old = m_s[rows, :]
    top = old
    for g in range(KB // HD):
        top = jnp.maximum(top, scores[:, head_cols(g)])
    keep = jnp.exp2((old - top) * EXP_SCALE)
    total = l_s[rows, :] * keep
    weighted = w_s[rows, :] * keep
    for g in range(KB // HD):
        e = jnp.exp2((scores[:, head_cols(g)] - top) * EXP_SCALE)
        if mask is not None:
            e = jnp.where(mask[:, head_cols(g)], e, 0.0)
        total = total + e
        weighted = weighted + e * dprobs[:, head_cols(g)]
    m_s[rows, :] = top
    l_s[rows, :] = total
    w_s[rows, :] = weighted


def cache_loop(info_ref, first, count, core, body):
    @pl.loop(0, count)
    def _(n):
        start = source_at(info_ref, first + n) * (2 * KB) + core * KB

        @pl.when((start + KB > info_ref[FLOOR]) & (start < info_ref[FLOOR]))
        def _():
            body(n, start, True)

        @pl.when(start >= info_ref[FLOOR])
        def _():
            body(n, start, False)


def pipelined(dots, rest):
    ready = dots(0)
    for r in range(CHUNKS):
        following = dots(r + 1) if r + 1 < CHUNKS else None
        rest(r, *ready)
        ready = following


def stats_kernel(first, groups, last, info_ref, *refs):
    refs = list(refs)
    flat = [refs.pop(0) for _ in range(sum(groups))]
    pieces = []
    for size in groups:
        pieces.append([flat.pop(0) for _ in range(size)])
    core = info_ref[CORE]
    if first == 0:
        q_ref, do_ref, pair_q_ref, pair_do_ref, gain_ref = refs[:5]
        q_s, do_s, m_s, l_s, w_s = refs[5:10]
        scratch = refs[10:]
        gain = gain_ref[...]
        for side, (raw_ref, grad_ref) in enumerate(((q_ref, do_ref), (pair_q_ref, pair_do_ref))):
            for h in range(HEADS):
                rows = slice((side * HEADS + h) * TOK, (side * HEADS + h + 1) * TOK)
                raw = raw_ref[:, head_cols(h)].astype(jnp.float32)
                q_s[rows, :] = unit_rows(raw, gain).astype(jnp.bfloat16)
                do_s[rows, :] = grad_ref[:, head_cols(h)]
        m_s[...] = jnp.full((ROWS, HD), NEG, jnp.float32)
        l_s[...] = jnp.zeros((ROWS, HD), jnp.float32)
        w_s[...] = jnp.zeros((ROWS, HD), jnp.float32)
    else:
        wins = []
        if last:
            wins = [refs.pop(0) for _ in range(CTX - 1)]
        q_s, do_s, m_in, l_in, w_in = refs[:5]
        if last:
            stat_ref, wk_ref, wv_ref = refs[5:8]
            m_s, l_s, w_s = refs[8:11]
            scratch = refs[11:]
        else:
            m_s, l_s, w_s = refs[5:8]
            scratch = refs[8:]
        m_s[...] = m_in[...]
        l_s[...] = l_in[...]
        w_s[...] = w_in[...]
    k_s, v_s = scratch
    place_cache(pieces, k_s, v_s)

    def body(n, start, masked):
        keys = k_s[keys_at(n), :]
        values = v_s[keys_at(n), :]
        mask = cache_mask(info_ref, start) if masked else None

        def dots(r):
            return (
                contract_last(q_s[chunk(r), :], keys),
                contract_last(do_s[chunk(r), :], values),
            )

        def rest(r, scores, dprobs):
            stat_block(scores, dprobs, mask, chunk(r), m_s, l_s, w_s)

        pipelined(dots, rest)

    cache_loop(info_ref, first, len(groups), core, body)
    if last:
        for n, piece in enumerate(wins + [pieces[-1][-1]]):
            at = pl.multiple_of(source(info_ref, *HOPS[n]) * HALF_WIN, HALF_WIN)
            low = piece.shape[0] - HALF_WIN
            wk_ref[pl.ds(at, HALF_WIN), :] = piece[low:, :HD]
            wv_ref[pl.ds(at, HALF_WIN), :] = piece[low:, HD:]

        win_mask = window_mask(info_ref)
        win_keys = wk_ref[...]
        win_values = wv_ref[...]

        def win_dots(r):
            return (
                contract_last(q_s[chunk(r), :], win_keys),
                contract_last(do_s[chunk(r), :], win_values),
            )

        def win_rest(r, scores, dprobs):
            stat_block(scores, dprobs, win_mask, chunk(r), m_s, l_s, w_s)

        pipelined(win_dots, win_rest)

        top = jnp.max(m_s[...], axis=1, keepdims=True)
        fix = jnp.exp2((m_s[...] - top) * EXP_SCALE)
        total = jnp.sum(l_s[...] * fix, axis=1, keepdims=True)
        weighted = jnp.sum(w_s[...] * fix, axis=1, keepdims=True)
        lane = lax.broadcasted_iota(jnp.int32, (ROWS, HD), 1)
        stat_ref[...] = jnp.where(lane == 0, top, jnp.where(lane == 1, total, weighted))


def stats_call(first, info, groups, rest, last=False):
    pieces = [piece for group in groups for piece in group]
    if first == 0:
        out = [SHAPE((ROWS, HD), jnp.bfloat16)] * 2 + STATE
    elif last:
        out = [SHAPE((ROWS, HD), jnp.float32)] + [SHAPE((KB, HD), jnp.bfloat16)] * 2
    else:
        out = STATE
    keys = len(groups) * KB
    scratch = [pltpu.VMEM((keys, HD), jnp.bfloat16)] * 2
    if last:
        scratch = [pltpu.VMEM((ROWS, HD), jnp.float32)] * 3 + scratch
    return pl.pallas_call(
        functools.partial(stats_kernel, first, [len(group) for group in groups], last),
        out_shape=out,
        in_specs=[SM] + [VM] * (len(pieces) + len(rest)),
        out_specs=[VM] * len(out),
        scratch_shapes=scratch,
        compiler_params=pltpu.CompilerParams(vmem_limit_bytes=VMEM_LIMIT),
        cost_estimate=block_cost(len(groups) + (1 if last else 0), 2),
        name="stats_" + str(first),
    )(info, *pieces, *rest)


def grad_block(scores, dprobs, mask, lse, delta):
    probs = []
    dscores = []
    for g in range(KB // HD):
        p = jnp.exp2(scores[:, head_cols(g)] * EXP_SCALE - lse)
        if mask is not None:
            p = jnp.where(mask[:, head_cols(g)], p, 0.0)
        probs.append(p.astype(jnp.bfloat16))
        dscores.append((p * (dprobs[:, head_cols(g)] - delta)).astype(jnp.bfloat16))
    return jnp.concatenate(probs, 1), jnp.concatenate(dscores, 1)


def window_kernel(
    info_ref, mine_ref, pair_ref, q_s, do_s, wk_ref, wv_ref, lse_ref, delta_ref, dq_ref, *rest
):
    parts, dkv_ref = rest[:4], rest[4]
    mine = mine_ref[...]
    half = ROWS // 2
    pair = jnp.concatenate([pair_ref[half:, :], pair_ref[:half, :]], 0)
    top = jnp.maximum(mine[:, 0:1], pair[:, 0:1])
    fix = jnp.exp2((mine[:, 0:1] - top) * EXP_SCALE)
    pair_fix = jnp.exp2((pair[:, 0:1] - top) * EXP_SCALE)
    total = mine[:, 1:2] * fix + pair[:, 1:2] * pair_fix
    weighted = mine[:, 2:3] * fix + pair[:, 2:3] * pair_fix
    lse_ref[...] = jnp.broadcast_to(top * EXP_SCALE + jnp.log2(total), (ROWS, HD))
    delta_ref[...] = jnp.broadcast_to(weighted / total, (ROWS, HD))
    dkv_ref[...] = jnp.zeros((KB, 2 * HD), jnp.float32)

    mask = window_mask(info_ref)
    keys = wk_ref[...]
    values = wv_ref[...]

    def dots(r):
        return contract_last(q_s[chunk(r), :], keys), contract_last(do_s[chunk(r), :], values)

    def rest(r, scores, dprobs):
        rows = chunk(r)
        probs, dscores = grad_block(scores, dprobs, mask, lse_ref[rows, :], delta_ref[rows, :])
        dq_ref[rows, :] = jnp.dot(dscores, keys, preferred_element_type=jnp.float32)
        dkv_ref[:, :HD] += contract_first(dscores, q_s[rows, :])
        dkv_ref[:, HD:] += contract_first(probs, do_s[rows, :])

    pipelined(dots, rest)

    for dz in range(4):
        at = pl.multiple_of(lax.bitwise_and(info_ref[Z] + dz, 3) * TOK, TOK)
        parts[dz][...] = dkv_ref[pl.ds(at, TOK), :]


def window_call(info, mine, pair, query, dout, win_k, win_v):
    out = STATE + [SHAPE((TOK, 2 * HD), jnp.float32)] * 4
    return pl.pallas_call(
        window_kernel,
        out_shape=out,
        in_specs=[SM] + [VM] * 6,
        out_specs=[VM] * 7,
        scratch_shapes=[pltpu.VMEM((KB, 2 * HD), jnp.float32)],
        compiler_params=pltpu.CompilerParams(vmem_limit_bytes=VMEM_LIMIT),
        cost_estimate=block_cost(1, 5),
        name="window_grads",
    )(info, mine, pair, query, dout, win_k, win_v)


def fetches(info_ref, weights, w_ref, kv_ref, sems):
    wq_ref, wk_ref, wv_ref, pair_wq_ref, pair_wk_ref, pair_wv_ref = weights
    copies = []
    for j in range(CHIPS):
        rows = pl.ds(pl.multiple_of((2 * j + info_ref[CORE]) * FEAT, FEAT), FEAT)
        for n, ref in enumerate((wq_ref, pair_wq_ref)):
            target = w_ref.at[j, :, pl.ds(n * COLS, COLS)]
            copies.append(pltpu.make_async_copy(ref.at[rows, :], target, sems.at[j, n]))
        for n, ref in enumerate((wk_ref, wv_ref, pair_wk_ref, pair_wv_ref)):
            target = kv_ref.at[j, pl.ds(n * SIDE, SIDE), :]
            copies.append(pltpu.make_async_copy(ref.at[:, rows], target, sems.at[j, 2 + n]))
    return copies


def cache_kernel(first, groups, info_ref, *refs):
    refs = list(refs)
    copies = []
    if first == 0:
        sems = refs.pop()
        weights = [refs.pop(0) for _ in range(6)]
        w_ref, kv_ref = refs[-4], refs[-3]
        del refs[-4:-2]
        copies = fetches(info_ref, weights, w_ref, kv_ref, sems)
    for copy in copies:
        copy.start()
    pieces = []
    for size in groups:
        pieces.append([refs.pop(0) for _ in range(size)])
    q_s, do_s, lse_ref, delta_ref, dq_in, dq_ref, k_s, v_s = refs
    place_cache(pieces, k_s, v_s)
    dq_ref[...] = dq_in[...]

    def body(n, start, masked):
        keys = k_s[keys_at(n), :]
        values = v_s[keys_at(n), :]
        mask = cache_mask(info_ref, start) if masked else None

        def dots(r):
            return contract_last(q_s[chunk(r), :], keys), contract_last(do_s[chunk(r), :], values)

        def rest(r, scores, dprobs):
            rows = chunk(r)
            _, dscores = grad_block(scores, dprobs, mask, lse_ref[rows, :], delta_ref[rows, :])
            dq_ref[rows, :] += jnp.dot(dscores, keys, preferred_element_type=jnp.float32)

        pipelined(dots, rest)

    cache_loop(info_ref, first, len(groups), info_ref[CORE], body)
    for copy in copies:
        copy.wait()


def cache_call(first, info, groups, query, dout, lse, delta, dq, weights=()):
    pieces = [piece for group in groups for piece in group]
    out = STATE[:1]
    scratch = [pltpu.VMEM((len(groups) * KB, HD), jnp.bfloat16)] * 2
    if weights:
        out = out + [
            SHAPE((CHIPS, FEAT, 2 * COLS), jnp.bfloat16),
            SHAPE((CHIPS, 2 * HD, FEAT), jnp.bfloat16),
        ]
        scratch = scratch + [pltpu.SemaphoreType.DMA((CHIPS, 6))]
    return pl.pallas_call(
        functools.partial(cache_kernel, first, [len(group) for group in groups]),
        out_shape=out,
        in_specs=[SM] + [HB] * len(weights) + [VM] * (len(pieces) + 5),
        out_specs=[VM] * len(out),
        scratch_shapes=scratch,
        compiler_params=pltpu.CompilerParams(vmem_limit_bytes=VMEM_LIMIT),
        cost_estimate=block_cost(len(groups), 3),
        name="cache_grads_" + str(first),
    )(info, *weights, *pieces, query, dout, lse, delta, dq)


def sum_kernel(info_ref, a_ref, b_ref, c_ref, d_ref, keep_ref, send_ref):
    total = (a_ref[...] + b_ref[...]) + (c_ref[...] + d_ref[...])
    first = info_ref[XH] == 0
    keep_ref[...] = jnp.where(first, total[:HALF_WIN, :], total[HALF_WIN:, :])
    send_ref[...] = jnp.where(first, total[HALF_WIN:, :], total[:HALF_WIN, :])


def sum_parts(info, parts):
    return pl.pallas_call(
        sum_kernel,
        out_shape=[SHAPE((HALF_WIN, 2 * HD), jnp.float32)] * 2,
        in_specs=[SM] + [VM] * 4,
        out_specs=[VM] * 2,
        compiler_params=SMALL,
        name="sum_parts",
    )(info, *parts)


def own_kv_kernel(idx_ref, keep_ref, other_ref, raw_ref, gain_ref, out_ref):
    total = keep_ref[...] + other_ref[...]
    raw = raw_ref[...].astype(jnp.float32)
    out_ref[:, :HD] = unit_back(raw, gain_ref[...], total[:, :HD] * SCALE).astype(jnp.bfloat16)
    out_ref[:, HD:] = total[:, HD:].astype(jnp.bfloat16)


def own_kv(idx, keep, other, k_raw, gain):
    def whole(i, idx):
        return (0, 0)

    return pl.pallas_call(
        own_kv_kernel,
        out_shape=SHAPE((HALF_WIN, 2 * HD), jnp.bfloat16),
        grid_spec=pltpu.PrefetchScalarGridSpec(
            num_scalar_prefetch=1,
            grid=(1,),
            in_specs=[
                pl.BlockSpec((HALF_WIN, 2 * HD), whole),
                pl.BlockSpec((HALF_WIN, 2 * HD), whole),
                pl.BlockSpec((HALF_WIN, HD), lambda i, idx: (idx[CORE], idx[CHIP])),
                pl.BlockSpec((1, HD), whole),
            ],
            out_specs=pl.BlockSpec((HALF_WIN, 2 * HD), whole),
        ),
        compiler_params=SMALL,
        name="own_kv",
    )(idx, keep, other, k_raw, gain)


def project_kernel(
    info_ref,
    dq_ref,
    pair_dq_ref,
    q_ref,
    pair_q_ref,
    gain_ref,
    kv_ref,
    pair_kv_ref,
    w_ref,
    wkv_ref,
    out_ref,
    g_s,
):
    core = info_ref[CORE]
    gain = gain_ref[...]
    for h in range(HEADS):
        rows = head_rows(h)
        low = slice(ROWS // 2 + h * TOK, ROWS // 2 + (h + 1) * TOK)
        for side, raw_ref, grad in (
            (0, q_ref, dq_ref[rows, :] + pair_dq_ref[low, :]),
            (1, pair_q_ref, dq_ref[low, :] + pair_dq_ref[rows, :]),
        ):
            raw = raw_ref[:, head_cols(h)].astype(jnp.float32)
            at = side * COLS + h * HD
            g_s[at : at + HD, :] = unit_back(raw, gain, grad * SCALE).T.astype(jnp.bfloat16)
    here = kv_ref[...].astype(jnp.float32)
    there = pair_kv_ref[...].astype(jnp.float32)
    top = jnp.where(core == 0, here, there)
    bottom = jnp.where(core == 0, there, here)
    kv = jnp.concatenate([top, bottom], 0)
    for n in range(2):
        both = kv[:, n * HD : (n + 1) * HD].T.astype(jnp.bfloat16)
        first = jnp.where(core == 0, both[:SIDE, :], both[SIDE:, :])
        second = jnp.where(core == 0, both[SIDE:, :], both[:SIDE, :])
        g_s[2 * COLS + n * SIDE : 2 * COLS + (n + 1) * SIDE, :] = first
        g_s[2 * COLS + (2 + n) * SIDE : 2 * COLS + (3 + n) * SIDE, :] = second
    for j in range(CHIPS):
        total = contract_first(wkv_ref[j], g_s[2 * COLS :, :])
        total += jnp.dot(w_ref[j], g_s[: 2 * COLS, :], preferred_element_type=jnp.float32)
        out_ref[j] = total.astype(jnp.bfloat16)


def project(info, *operands):
    return pl.pallas_call(
        project_kernel,
        out_shape=SHAPE((CHIPS, FEAT, TOK), jnp.bfloat16),
        in_specs=[SM] + [VM] * 9,
        out_specs=VM,
        scratch_shapes=[pltpu.VMEM((2 * COLS + 2 * HD, TOK), jnp.bfloat16)],
        compiler_params=pltpu.CompilerParams(vmem_limit_bytes=VMEM_LIMIT),
        cost_estimate=cost(2 * TOK * D // 2 * 1280, 0, 12e6),
        name="project",
    )(info, *operands)


def rows_kernel(pieces_ref, resid_ref, dh_ref, grad_ref, sums_ref):
    inner = jnp.zeros((1, TOK), jnp.float32)
    square = jnp.zeros((1, TOK), jnp.float32)
    for n in range(FEAT // HD):
        rows = head_cols(n)
        grad = pieces_ref[0, rows, :].astype(jnp.float32)
        for m in range(1, CHIPS):
            grad += pieces_ref[m, rows, :].astype(jnp.float32)
        grad += dh_ref[rows, :].astype(jnp.float32)
        grad_ref[rows, :] = grad
        resid = resid_ref[rows, :].astype(jnp.float32)
        inner += jnp.sum(grad * resid, axis=0, keepdims=True)
        square += jnp.sum(resid * resid, axis=0, keepdims=True)
    row = lax.broadcasted_iota(jnp.int32, (8, TOK), 0)
    sums_ref[...] = jnp.where(row == 0, inner, square)


def row_sums(pieces, resid_t, dh_t):
    return pl.pallas_call(
        rows_kernel,
        out_shape=[SHAPE((FEAT, TOK), jnp.float32), SHAPE((8, TOK), jnp.float32)],
        in_specs=[VM] * 3,
        out_specs=[VM] * 2,
        compiler_params=SMALL,
        name="row_sums",
    )(pieces, resid_t, dh_t)


def norm_kernel(grad_ref, sums_ref, resid_ref, out_ref):
    sums = sums_ref[0]
    for n in range(1, 2 * CHIPS):
        sums += sums_ref[n]
    mean_sq = sums[1:2, :] / D
    factor = lax.rsqrt(mean_sq + EPS) / math.sqrt(D)
    correction = sums[0:1, :] / (D * (mean_sq + EPS))
    for n in range(FEAT // HD):
        rows = head_cols(n)
        resid = resid_ref[rows, :].astype(jnp.float32)
        out_ref[:, rows] = (factor * (grad_ref[rows, :] - resid * correction)).T


def last_norm(grad_t, sums, resid_t):
    return pl.pallas_call(
        norm_kernel,
        out_shape=SHAPE((TOK, FEAT), jnp.float32),
        in_specs=[VM] * 3,
        out_specs=VM,
        compiler_params=SMALL,
        name="last_norm",
    )(grad_t, sums, resid_t)


def shift(block, axis, by):
    count = lax.axis_size(axis)
    return lax.ppermute(block, axis, [(i, (i + by) % count) for i in range(count)])


def swap(block, axis):
    return shift(block, axis, 1)


def on_device(
    residual_in,
    dh_rest,
    w_query,
    w_key,
    w_value,
    q_raw,
    k_raw,
    v_win,
    cache_k,
    cache_v,
    d_attn,
    s_qk,
    cache_live,
):
    info = jnp.stack(
        [
            lax.axis_index("z"),
            lax.axis_index("xh"),
            lax.axis_index("xl") * 4 + lax.axis_index("y"),
            lax.axis_index("c"),
            CACHE - cache_live[0],
        ]
    ).astype(jnp.int32)
    gain = s_qk.reshape(1, HD)

    sources = [cache_k, cache_v, k_raw, v_win, residual_in, dh_rest]
    sources = [pltpu.with_memory_space_constraint(array, pltpu.HBM) for array in sources]
    here, resid_t, dh_t = pack_rows(info, *sources, gain)
    there = swap(here, "xh")
    up = shift(here, "z", -1)
    down = shift(here, "z", 1)
    pair_wide = swap(w_query, "c")
    pair_q = swap(q_raw, "c")
    pair_do = swap(d_attn, "c")
    up_there = shift(there, "z", -1)
    down_there = shift(there, "z", 1)
    far = [shift(up[:CUT], "z", -1), shift(down[CUT:], "z", 1)]
    groups = [[here], [there], [up], [down]]
    query, dout, *state = stats_call(
        0, info, groups[:4], [q_raw, d_attn, pair_q, pair_do, gain]
    )
    query, dout, state, up_there, down_there = lax.optimization_barrier(
        (query, dout, state, up_there, down_there)
    )
    far_there = [shift(up_there[:CUT], "z", -1), shift(down_there[CUT:], "z", 1)]
    groups += [[up_there], [down_there], far, far_there]
    state = stats_call(4, info, groups[4:7], [query, dout, *state])
    narrow = [w_key.T, w_value.T]
    state, narrow = lax.optimization_barrier((state, narrow))
    weights = [w_query, *narrow]
    pair_weights = [pair_wide] + [swap(w, "c") for w in narrow]
    wins = [group[-1] for group in groups[:-1]]
    stat, win_k, win_v = stats_call(
        7, info, groups[7:], wins + [query, dout, *state], last=True
    )
    pair_stat, pair_weights = lax.optimization_barrier((swap(stat, "c"), pair_weights))
    lse, delta, dq, *parts = window_call(info, stat, pair_stat, query, dout, win_k, win_v)
    parts = [parts[0]] + [shift(parts[dz], "z", dz) for dz in (1, 3, 2)]
    dq, w_own, w_kv = cache_call(
        0, info, groups[:5], query, dout, lse, delta, dq, [*weights, *pair_weights]
    )
    parts, dq = lax.optimization_barrier((parts, dq))
    keep, send = sum_parts(info, parts)
    other = swap(send, "xh")
    (dq,) = cache_call(5, info, groups[5:], query, dout, lse, delta, dq)
    other, dq = lax.optimization_barrier((other, dq))
    pair_dq = swap(dq, "c")
    kv = own_kv(info, keep, other, k_raw, gain)
    pair_kv = swap(kv, "c")
    partial = project(info, dq, pair_dq, q_raw, pair_q, gain, kv, pair_kv, w_own, w_kv)
    pieces = lax.all_to_all(partial, CHIP_AXES, 0, 0)
    grad_t, sums = row_sums(pieces, resid_t, dh_t)
    everyone = lax.all_to_all(
        jnp.broadcast_to(sums[None], (2 * CHIPS, 8, TOK)), TP_AXES, 0, 0
    )
    return last_norm(grad_t, everyone, resid_t)


def solution(mesh):
    fine = Mesh(mesh.devices.reshape(4, 2, 2, 4, 2), ("z", "xh", "xl", "y", "c"))
    both = P(CTX_AXES, TP_AXES)
    cols = P(None, TP_AXES)
    rows = P(CTX_AXES, None)
    return jax.shard_map(
        on_device,
        mesh=fine,
        in_specs=(both, both, cols, cols, cols, both, rows, rows, rows, rows, both, P(), P()),
        out_specs=both,
        check_vma=False,
    )
```

```python
import functools
import math

import jax
import jax.numpy as jnp
from jax import lax
from jax.experimental import pallas as pl
from jax.experimental.pallas import tpu as pltpu
from jax.sharding import Mesh
from jax.sharding import PartitionSpec as P

D = 8192
KVH = 8
HD = 128
CACHE = 8192
TOKENS = 1024
CTX = 8
TOK = TOKENS // CTX
HEADS = 4
ROWS = 2 * HEADS * TOK
COLS = HEADS * HD
SIDE = HD // 2
CHIPS = 8
FEAT = D // 16
HALF_CACHE = CACHE // CTX // 2
HALF_WIN = TOK // 2
HALF = HALF_CACHE + HALF_WIN
KB = 512
CHUNK = 512
CHUNKS = ROWS // CHUNK
EPS = 1e-06
SCALE = math.sqrt(HD)
EXP_SCALE = SCALE * math.log2(math.e)
NEG = -1e30
VMEM_LIMIT = 24 * 1024 * 1024
TP_AXES = ("xl", "y", "c")
CTX_AXES = ("z", "xh")
CHIP_AXES = ("xl", "y")


HOPS = ((0, 0), (0, 1), (1, 0), (3, 0), (1, 1), (3, 1), (2, 0), (2, 1))
Z, XH, CHIP, CORE, FLOOR = range(5)
SHAPE = jax.ShapeDtypeStruct
STATE = [SHAPE((ROWS, HD), jnp.float32)] * 3
VM = pl.BlockSpec(memory_space=pltpu.VMEM)
SM = pl.BlockSpec(memory_space=pltpu.SMEM)
HB = pl.BlockSpec(memory_space=pltpu.HBM)
SMALL = pltpu.CompilerParams(vmem_limit_bytes=8 * 1024 * 1024)


def contract_last(left, right):
    return lax.dot_general(
        left, right, (((1,), (1,)), ((), ())), preferred_element_type=jnp.float32
    )


def contract_first(left, right):
    return lax.dot_general(
        left, right, (((0,), (0,)), ((), ())), preferred_element_type=jnp.float32
    )


def unit_rows(values, qk_gain):
    width = values.shape[-1]
    mean_sq = jnp.mean(values * values, axis=-1, keepdims=True)
    return values * (lax.rsqrt(mean_sq + EPS) / math.sqrt(width)) * qk_gain


def unit_back(values, qk_gain, grad):
    width = values.shape[-1]
    mean_sq = jnp.mean(values * values, axis=-1, keepdims=True)
    factor = lax.rsqrt(mean_sq + EPS) / math.sqrt(width)
    weighted = qk_gain * grad
    inner = jnp.sum(weighted * values, axis=-1, keepdims=True)
    return factor * (weighted - values * inner / (width * (mean_sq + EPS)))


def head_cols(h):
    return slice(h * HD, (h + 1) * HD)


def head_rows(h):
    return slice(h * TOK, (h + 1) * TOK)


def pack_kernel(
    info_ref,
    ck_ref,
    cv_ref,
    kr_ref,
    vw_ref,
    resid_ref,
    dh_ref,
    q_ref,
    do_ref,
    gain_ref,
    out_ref,
    resid_out,
    dh_out,
    q_out,
    do_out,
    ck_s,
    kr_s,
    resid_s,
    dh_s,
    sems,
):
    cols = pl.ds(pl.multiple_of(info_ref[CHIP] * HD, HD), HD)
    cache = pl.ds(pl.multiple_of(info_ref[CORE] * HALF_CACHE, HALF_CACHE), HALF_CACHE)
    win = pl.ds(pl.multiple_of(info_ref[CORE] * HALF_WIN, HALF_WIN), HALF_WIN)
    right = pl.ds(HD, HD)
    copies = [
        pltpu.make_async_copy(ck_ref.at[cache, cols], ck_s, sems.at[0]),
        pltpu.make_async_copy(kr_ref.at[win, cols], kr_s, sems.at[1]),
        pltpu.make_async_copy(
            cv_ref.at[cache, cols], out_ref.at[pl.ds(0, HALF_CACHE), right], sems.at[2]
        ),
        pltpu.make_async_copy(
            vw_ref.at[win, cols], out_ref.at[pl.ds(HALF_CACHE, HALF_WIN), right], sems.at[3]
        ),
        pltpu.make_async_copy(resid_ref, resid_s, sems.at[4]),
        pltpu.make_async_copy(dh_ref, dh_s, sems.at[5]),
        pltpu.make_async_copy(q_ref, q_out, sems.at[6]),
        pltpu.make_async_copy(do_ref, do_out, sems.at[7]),
    ]
    for copy in copies:
        copy.start()
    gain = gain_ref[...]
    copies[0].wait()
    out_ref[:HALF_CACHE, :HD] = unit_rows(ck_s[...].astype(jnp.float32), gain).astype(jnp.bfloat16)
    copies[1].wait()
    out_ref[HALF_CACHE:, :HD] = unit_rows(kr_s[...].astype(jnp.float32), gain).astype(jnp.bfloat16)
    copies[2].wait()
    copies[3].wait()
    copies[4].wait()
    resid_out[...] = resid_s[...].astype(jnp.float32).T.astype(jnp.bfloat16)
    copies[5].wait()
    dh_out[...] = dh_s[...].astype(jnp.float32).T.astype(jnp.bfloat16)
    copies[6].wait()
    copies[7].wait()


def pack_rows(info, *operands):
    return pl.pallas_call(
        pack_kernel,
        out_shape=[
            SHAPE((HALF, 2 * HD), jnp.bfloat16),
            SHAPE((FEAT, TOK), jnp.bfloat16),
            SHAPE((FEAT, TOK), jnp.bfloat16),
            SHAPE((TOK, COLS), jnp.bfloat16),
            SHAPE((TOK, COLS), jnp.bfloat16),
        ],
        in_specs=[SM] + [HB] * 8 + [VM],
        out_specs=[VM] * 5,
        scratch_shapes=[
            pltpu.VMEM((HALF_CACHE, HD), jnp.bfloat16),
            pltpu.VMEM((HALF_WIN, HD), jnp.bfloat16),
            pltpu.VMEM((TOK, FEAT), jnp.bfloat16),
            pltpu.VMEM((TOK, FEAT), jnp.bfloat16),
            pltpu.SemaphoreType.DMA((8,)),
        ],
        compiler_params=SMALL,
        name="pack_rows",
    )(info, *operands)


def cost(flops, exps, moved):
    return pl.CostEstimate(
        flops=int(flops), transcendentals=int(exps), bytes_accessed=int(moved)
    )


def block_cost(blocks, dots):
    return cost(
        blocks * dots * 2 * ROWS * KB * HD, blocks * ROWS * KB, blocks * 4 * KB * HD + 2 ** 21
    )


def source(info_ref, dz, dx):
    return lax.bitwise_and(info_ref[Z] + dz, 3) * 2 + lax.bitwise_and(info_ref[XH] + dx, 1)


def source_at(info_ref, n):
    dz = jnp.where(n >= 6, 2, jnp.where(n < 2, 0, jnp.where(lax.bitwise_and(n, 1) == 0, 1, 3)))
    dx = jnp.where(n >= 6, n - 6, jnp.where(n < 2, n, jnp.where(n >= 4, 1, 0)))
    return source(info_ref, dz, dx)


def cache_mask(info_ref, start):
    return start + lax.broadcasted_iota(jnp.int32, (CHUNK, KB), 1) >= info_ref[FLOOR]


def window_mask(info_ref):
    local = lax.broadcasted_iota(jnp.int32, (CHUNK, KB), 1)
    key = (
        lax.shift_right_logical(local, 6) * TOK
        + info_ref[CORE] * HALF_WIN
        + lax.bitwise_and(local, jnp.int32(HALF_WIN - 1))
    )
    token = source(info_ref, 0, 0) * TOK + lax.bitwise_and(
        lax.broadcasted_iota(jnp.int32, (CHUNK, KB), 0), jnp.int32(TOK - 1)
    )
    return key <= token


def chunk(r):
    return slice(r * CHUNK, (r + 1) * CHUNK)


def keys_at(n):
    return pl.ds(pl.multiple_of(n * KB, KB), KB)


def place_cache(pieces, k_s, v_s, at=0):
    for n, group in enumerate(pieces):
        row = (at + n) * KB
        for piece in group:
            rows = min(piece.shape[0], (at + n + 1) * KB - row)
            k_s[row : row + rows, :] = piece[:rows, :HD]
            v_s[row : row + rows, :] = piece[:rows, HD:]
            row += rows


def stat_block(scores, dprobs, mask, rows, m_s, l_s, w_s):
    if mask is not None:
        scores = jnp.where(mask, scores, NEG)
    old = m_s[rows, :]
    top = old
    for g in range(KB // HD):
        top = jnp.maximum(top, scores[:, head_cols(g)])
    keep = jnp.exp2((old - top) * EXP_SCALE)
    total = l_s[rows, :] * keep
    weighted = w_s[rows, :] * keep
    for g in range(KB // HD):
        e = jnp.exp2((scores[:, head_cols(g)] - top) * EXP_SCALE)
        if mask is not None:
            e = jnp.where(mask[:, head_cols(g)], e, 0.0)
        total = total + e
        weighted = weighted + e * dprobs[:, head_cols(g)]
    m_s[rows, :] = top
    l_s[rows, :] = total
    w_s[rows, :] = weighted


def cache_loop(info_ref, first, count, core, body):
    @pl.loop(0, count)
    def _(n):
        start = source_at(info_ref, first + n) * (2 * KB) + core * KB

        @pl.when((start + KB > info_ref[FLOOR]) & (start < info_ref[FLOOR]))
        def _():
            body(n, start, True)

        @pl.when(start >= info_ref[FLOOR])
        def _():
            body(n, start, False)


def pipelined(dots, rest):
    ready = dots(0)
    for r in range(CHUNKS):
        following = dots(r + 1) if r + 1 < CHUNKS else None
        rest(r, *ready)
        ready = following


def stats_kernel(first, groups, last, info_ref, *refs):
    refs = list(refs)
    flat = [refs.pop(0) for _ in range(sum(groups))]
    pieces = []
    for size in groups:
        pieces.append([flat.pop(0) for _ in range(size)])
    core = info_ref[CORE]
    if first == 0:
        q_ref, do_ref, pair_q_ref, pair_do_ref, gain_ref = refs[:5]
        q_s, do_s, m_s, l_s, w_s = refs[5:10]
        scratch = refs[10:]
        gain = gain_ref[...]
        for side, (raw_ref, grad_ref) in enumerate(((q_ref, do_ref), (pair_q_ref, pair_do_ref))):
            for h in range(HEADS):
                rows = slice((side * HEADS + h) * TOK, (side * HEADS + h + 1) * TOK)
                raw = raw_ref[:, head_cols(h)].astype(jnp.float32)
                q_s[rows, :] = unit_rows(raw, gain).astype(jnp.bfloat16)
                do_s[rows, :] = grad_ref[:, head_cols(h)]
        m_s[...] = jnp.full((ROWS, HD), NEG, jnp.float32)
        l_s[...] = jnp.zeros((ROWS, HD), jnp.float32)
        w_s[...] = jnp.zeros((ROWS, HD), jnp.float32)
    else:
        wins = []
        if last:
            wins = [refs.pop(0) for _ in range(first)]
        q_s, do_s, m_in, l_in, w_in = refs[:5]
        if last:
            stat_ref, wk_ref, wv_ref = refs[5:8]
            m_s, l_s, w_s = refs[8:11]
            scratch = refs[11:]
        else:
            m_s, l_s, w_s = refs[5:8]
            scratch = refs[8:]
        m_s[...] = m_in[...]
        l_s[...] = l_in[...]
        w_s[...] = w_in[...]
    k_s, v_s = scratch
    place_cache(pieces, k_s, v_s)

    def body(n, start, masked):
        keys = k_s[keys_at(n), :]
        values = v_s[keys_at(n), :]
        mask = cache_mask(info_ref, start) if masked else None

        def dots(r):
            return (
                contract_last(q_s[chunk(r), :], keys),
                contract_last(do_s[chunk(r), :], values),
            )

        def rest(r, scores, dprobs):
            stat_block(scores, dprobs, mask, chunk(r), m_s, l_s, w_s)

        pipelined(dots, rest)

    cache_loop(info_ref, first, len(groups), core, body)
    if last:
        for n, piece in enumerate(wins + [group[-1] for group in pieces]):
            at = pl.multiple_of(source(info_ref, *HOPS[n]) * HALF_WIN, HALF_WIN)
            low = piece.shape[0] - HALF_WIN
            wk_ref[pl.ds(at, HALF_WIN), :] = piece[low:, :HD]
            wv_ref[pl.ds(at, HALF_WIN), :] = piece[low:, HD:]

        win_mask = window_mask(info_ref)
        win_keys = wk_ref[...]
        win_values = wv_ref[...]

        def win_dots(r):
            return (
                contract_last(q_s[chunk(r), :], win_keys),
                contract_last(do_s[chunk(r), :], win_values),
            )

        def win_rest(r, scores, dprobs):
            stat_block(scores, dprobs, win_mask, chunk(r), m_s, l_s, w_s)

        pipelined(win_dots, win_rest)

        top = jnp.max(m_s[...], axis=1, keepdims=True)
        fix = jnp.exp2((m_s[...] - top) * EXP_SCALE)
        total = jnp.sum(l_s[...] * fix, axis=1, keepdims=True)
        weighted = jnp.sum(w_s[...] * fix, axis=1, keepdims=True)
        lane = lax.broadcasted_iota(jnp.int32, (ROWS, HD), 1)
        stat_ref[...] = jnp.where(lane == 0, top, jnp.where(lane == 1, total, weighted))


def stats_call(first, info, groups, rest, last=False):
    pieces = [piece for group in groups for piece in group]
    if first == 0:
        out = [SHAPE((ROWS, HD), jnp.bfloat16)] * 2 + STATE
    elif last:
        out = [SHAPE((ROWS, HD), jnp.float32)] + [SHAPE((KB, HD), jnp.bfloat16)] * 2
    else:
        out = STATE
    keys = len(groups) * KB
    scratch = [pltpu.VMEM((keys, HD), jnp.bfloat16)] * 2
    if last:
        scratch = [pltpu.VMEM((ROWS, HD), jnp.float32)] * 3 + scratch
    return pl.pallas_call(
        functools.partial(stats_kernel, first, [len(group) for group in groups], last),
        out_shape=out,
        in_specs=[SM] + [VM] * (len(pieces) + len(rest)),
        out_specs=[VM] * len(out),
        scratch_shapes=scratch,
        compiler_params=pltpu.CompilerParams(vmem_limit_bytes=VMEM_LIMIT),
        cost_estimate=block_cost(len(groups) + (1 if last else 0), 2),
        name="stats_" + str(first),
    )(info, *pieces, *rest)


def grad_block(scores, dprobs, mask, lse, delta):
    probs = []
    dscores = []
    for g in range(KB // HD):
        p = jnp.exp2(scores[:, head_cols(g)] * EXP_SCALE - lse)
        if mask is not None:
            p = jnp.where(mask[:, head_cols(g)], p, 0.0)
        probs.append(p.astype(jnp.bfloat16))
        dscores.append((p * (dprobs[:, head_cols(g)] - delta)).astype(jnp.bfloat16))
    return jnp.concatenate(probs, 1), jnp.concatenate(dscores, 1)


def window_kernel(
    info_ref, mine_ref, pair_ref, q_s, do_s, wk_ref, wv_ref, lse_ref, delta_ref, dq_ref, *rest
):
    parts, dkv_ref = rest[:4], rest[4]
    mine = mine_ref[...]
    half = ROWS // 2
    pair = jnp.concatenate([pair_ref[half:, :], pair_ref[:half, :]], 0)
    top = jnp.maximum(mine[:, 0:1], pair[:, 0:1])
    fix = jnp.exp2((mine[:, 0:1] - top) * EXP_SCALE)
    pair_fix = jnp.exp2((pair[:, 0:1] - top) * EXP_SCALE)
    total = mine[:, 1:2] * fix + pair[:, 1:2] * pair_fix
    weighted = mine[:, 2:3] * fix + pair[:, 2:3] * pair_fix
    lse_ref[...] = jnp.broadcast_to(top * EXP_SCALE + jnp.log2(total), (ROWS, HD))
    delta_ref[...] = jnp.broadcast_to(weighted / total, (ROWS, HD))
    dkv_ref[...] = jnp.zeros((KB, 2 * HD), jnp.float32)

    mask = window_mask(info_ref)
    keys = wk_ref[...]
    values = wv_ref[...]

    def dots(r):
        return contract_last(q_s[chunk(r), :], keys), contract_last(do_s[chunk(r), :], values)

    def rest(r, scores, dprobs):
        rows = chunk(r)
        probs, dscores = grad_block(scores, dprobs, mask, lse_ref[rows, :], delta_ref[rows, :])
        dq_ref[rows, :] = jnp.dot(dscores, keys, preferred_element_type=jnp.float32)
        dkv_ref[:, :HD] += contract_first(dscores, q_s[rows, :])
        dkv_ref[:, HD:] += contract_first(probs, do_s[rows, :])

    pipelined(dots, rest)

    for dz in range(4):
        at = pl.multiple_of(lax.bitwise_and(info_ref[Z] + dz, 3) * TOK, TOK)
        parts[dz][...] = dkv_ref[pl.ds(at, TOK), :]


def window_call(info, mine, pair, query, dout, win_k, win_v):
    out = STATE + [SHAPE((TOK, 2 * HD), jnp.float32)] * 4
    return pl.pallas_call(
        window_kernel,
        out_shape=out,
        in_specs=[SM] + [VM] * 6,
        out_specs=[VM] * 7,
        scratch_shapes=[pltpu.VMEM((KB, 2 * HD), jnp.float32)],
        compiler_params=pltpu.CompilerParams(vmem_limit_bytes=VMEM_LIMIT),
        cost_estimate=block_cost(1, 5),
        name="window_grads",
    )(info, mine, pair, query, dout, win_k, win_v)


def fetches(info_ref, weights, w_ref, kv_ref, sems):
    wq_ref, wk_ref, wv_ref, pair_wq_ref, pair_wk_ref, pair_wv_ref = weights
    copies = []
    for j in range(CHIPS):
        rows = pl.ds(pl.multiple_of((2 * j + info_ref[CORE]) * FEAT, FEAT), FEAT)
        for n, ref in enumerate((wq_ref, pair_wq_ref)):
            target = w_ref.at[j, :, pl.ds(n * COLS, COLS)]
            copies.append(pltpu.make_async_copy(ref.at[rows, :], target, sems.at[j, n]))
        for n, ref in enumerate((wk_ref, wv_ref, pair_wk_ref, pair_wv_ref)):
            target = kv_ref.at[j, pl.ds(n * SIDE, SIDE), :]
            copies.append(pltpu.make_async_copy(ref.at[:, rows], target, sems.at[j, 2 + n]))
    return copies


def cache_kernel(first, groups, info_ref, *refs):
    refs = list(refs)
    copies = []
    if first == 0:
        sems = refs.pop()
        weights = [refs.pop(0) for _ in range(6)]
        w_ref, kv_ref = refs[-4], refs[-3]
        del refs[-4:-2]
        copies = fetches(info_ref, weights, w_ref, kv_ref, sems)
    for copy in copies:
        copy.start()
    pieces = []
    for size in groups:
        pieces.append([refs.pop(0) for _ in range(size)])
    q_s, do_s, lse_ref, delta_ref, dq_in, dq_ref, k_s, v_s = refs
    place_cache(pieces, k_s, v_s)
    dq_ref[...] = dq_in[...]

    def body(n, start, masked):
        keys = k_s[keys_at(n), :]
        values = v_s[keys_at(n), :]
        mask = cache_mask(info_ref, start) if masked else None

        def dots(r):
            return contract_last(q_s[chunk(r), :], keys), contract_last(do_s[chunk(r), :], values)

        def rest(r, scores, dprobs):
            rows = chunk(r)
            _, dscores = grad_block(scores, dprobs, mask, lse_ref[rows, :], delta_ref[rows, :])
            dq_ref[rows, :] += jnp.dot(dscores, keys, preferred_element_type=jnp.float32)

        pipelined(dots, rest)

    cache_loop(info_ref, first, len(groups), info_ref[CORE], body)
    for copy in copies:
        copy.wait()


def cache_call(first, info, groups, query, dout, lse, delta, dq, weights=()):
    pieces = [piece for group in groups for piece in group]
    out = STATE[:1]
    scratch = [pltpu.VMEM((len(groups) * KB, HD), jnp.bfloat16)] * 2
    if weights:
        out = out + [
            SHAPE((CHIPS, FEAT, 2 * COLS), jnp.bfloat16),
            SHAPE((CHIPS, 2 * HD, FEAT), jnp.bfloat16),
        ]
        scratch = scratch + [pltpu.SemaphoreType.DMA((CHIPS, 6))]
    return pl.pallas_call(
        functools.partial(cache_kernel, first, [len(group) for group in groups]),
        out_shape=out,
        in_specs=[SM] + [HB] * len(weights) + [VM] * (len(pieces) + 5),
        out_specs=[VM] * len(out),
        scratch_shapes=scratch,
        compiler_params=pltpu.CompilerParams(vmem_limit_bytes=VMEM_LIMIT),
        cost_estimate=block_cost(len(groups), 3),
        name="cache_grads_" + str(first),
    )(info, *weights, *pieces, query, dout, lse, delta, dq)


def sum_kernel(info_ref, a_ref, b_ref, c_ref, d_ref, keep_ref, send_ref):
    total = (a_ref[...] + b_ref[...]) + (c_ref[...] + d_ref[...])
    first = info_ref[XH] == 0
    keep_ref[...] = jnp.where(first, total[:HALF_WIN, :], total[HALF_WIN:, :])
    send_ref[...] = jnp.where(first, total[HALF_WIN:, :], total[:HALF_WIN, :])


def sum_parts(info, parts):
    return pl.pallas_call(
        sum_kernel,
        out_shape=[SHAPE((HALF_WIN, 2 * HD), jnp.float32)] * 2,
        in_specs=[SM] + [VM] * 4,
        out_specs=[VM] * 2,
        compiler_params=SMALL,
        name="sum_parts",
    )(info, *parts)


def own_kv_kernel(idx_ref, keep_ref, other_ref, raw_ref, gain_ref, out_ref):
    total = keep_ref[...] + other_ref[...]
    raw = raw_ref[...].astype(jnp.float32)
    out_ref[:, :HD] = unit_back(raw, gain_ref[...], total[:, :HD] * SCALE).astype(jnp.bfloat16)
    out_ref[:, HD:] = total[:, HD:].astype(jnp.bfloat16)


def own_kv(idx, keep, other, k_raw, gain):
    def whole(i, idx):
        return (0, 0)

    return pl.pallas_call(
        own_kv_kernel,
        out_shape=SHAPE((HALF_WIN, 2 * HD), jnp.bfloat16),
        grid_spec=pltpu.PrefetchScalarGridSpec(
            num_scalar_prefetch=1,
            grid=(1,),
            in_specs=[
                pl.BlockSpec((HALF_WIN, 2 * HD), whole),
                pl.BlockSpec((HALF_WIN, 2 * HD), whole),
                pl.BlockSpec((HALF_WIN, HD), lambda i, idx: (idx[CORE], idx[CHIP])),
                pl.BlockSpec((1, HD), whole),
            ],
            out_specs=pl.BlockSpec((HALF_WIN, 2 * HD), whole),
        ),
        compiler_params=SMALL,
        name="own_kv",
    )(idx, keep, other, k_raw, gain)


def project_kernel(
    info_ref,
    dq_ref,
    pair_dq_ref,
    q_ref,
    pair_q_ref,
    gain_ref,
    kv_ref,
    pair_kv_ref,
    w_ref,
    wkv_ref,
    out_ref,
    g_s,
):
    core = info_ref[CORE]
    gain = gain_ref[...]
    for h in range(HEADS):
        rows = head_rows(h)
        low = slice(ROWS // 2 + h * TOK, ROWS // 2 + (h + 1) * TOK)
        for side, raw_ref, grad in (
            (0, q_ref, dq_ref[rows, :] + pair_dq_ref[low, :]),
            (1, pair_q_ref, dq_ref[low, :] + pair_dq_ref[rows, :]),
        ):
            raw = raw_ref[:, head_cols(h)].astype(jnp.float32)
            at = side * COLS + h * HD
            g_s[at : at + HD, :] = unit_back(raw, gain, grad * SCALE).T.astype(jnp.bfloat16)
    here = kv_ref[...].astype(jnp.float32)
    there = pair_kv_ref[...].astype(jnp.float32)
    top = jnp.where(core == 0, here, there)
    bottom = jnp.where(core == 0, there, here)
    kv = jnp.concatenate([top, bottom], 0)
    for n in range(2):
        both = kv[:, n * HD : (n + 1) * HD].T.astype(jnp.bfloat16)
        first = jnp.where(core == 0, both[:SIDE, :], both[SIDE:, :])
        second = jnp.where(core == 0, both[SIDE:, :], both[:SIDE, :])
        g_s[2 * COLS + n * SIDE : 2 * COLS + (n + 1) * SIDE, :] = first
        g_s[2 * COLS + (2 + n) * SIDE : 2 * COLS + (3 + n) * SIDE, :] = second
    for j in range(CHIPS):
        total = contract_first(wkv_ref[j], g_s[2 * COLS :, :])
        total += jnp.dot(w_ref[j], g_s[: 2 * COLS, :], preferred_element_type=jnp.float32)
        out_ref[j] = total.astype(jnp.bfloat16)


def project(info, *operands):
    return pl.pallas_call(
        project_kernel,
        out_shape=SHAPE((CHIPS, FEAT, TOK), jnp.bfloat16),
        in_specs=[SM] + [VM] * 9,
        out_specs=VM,
        scratch_shapes=[pltpu.VMEM((2 * COLS + 2 * HD, TOK), jnp.bfloat16)],
        compiler_params=pltpu.CompilerParams(vmem_limit_bytes=VMEM_LIMIT),
        cost_estimate=cost(2 * TOK * D // 2 * 1280, 0, 12e6),
        name="project",
    )(info, *operands)


def rows_kernel(pieces_ref, resid_ref, dh_ref, grad_ref, sums_ref):
    inner = jnp.zeros((1, TOK), jnp.float32)
    square = jnp.zeros((1, TOK), jnp.float32)
    for n in range(FEAT // HD):
        rows = head_cols(n)
        grad = pieces_ref[0, rows, :].astype(jnp.float32)
        for m in range(1, CHIPS):
            grad += pieces_ref[m, rows, :].astype(jnp.float32)
        grad += dh_ref[rows, :].astype(jnp.float32)
        grad_ref[rows, :] = grad
        resid = resid_ref[rows, :].astype(jnp.float32)
        inner += jnp.sum(grad * resid, axis=0, keepdims=True)
        square += jnp.sum(resid * resid, axis=0, keepdims=True)
    row = lax.broadcasted_iota(jnp.int32, (8, TOK), 0)
    sums_ref[...] = jnp.where(row == 0, inner, square)


def row_sums(pieces, resid_t, dh_t):
    return pl.pallas_call(
        rows_kernel,
        out_shape=[SHAPE((FEAT, TOK), jnp.float32), SHAPE((8, TOK), jnp.float32)],
        in_specs=[VM] * 3,
        out_specs=[VM] * 2,
        compiler_params=SMALL,
        name="row_sums",
    )(pieces, resid_t, dh_t)


def norm_kernel(grad_ref, sums_ref, resid_ref, out_ref):
    sums = sums_ref[0]
    for n in range(1, 2 * CHIPS):
        sums += sums_ref[n]
    mean_sq = sums[1:2, :] / D
    factor = lax.rsqrt(mean_sq + EPS) / math.sqrt(D)
    correction = sums[0:1, :] / (D * (mean_sq + EPS))
    for n in range(FEAT // HD):
        rows = head_cols(n)
        resid = resid_ref[rows, :].astype(jnp.float32)
        out_ref[:, rows] = (factor * (grad_ref[rows, :] - resid * correction)).T


def last_norm(grad_t, sums, resid_t):
    return pl.pallas_call(
        norm_kernel,
        out_shape=SHAPE((TOK, FEAT), jnp.float32),
        in_specs=[VM] * 3,
        out_specs=VM,
        compiler_params=SMALL,
        name="last_norm",
    )(grad_t, sums, resid_t)


def shift(block, axis, by):
    count = lax.axis_size(axis)
    return lax.ppermute(block, axis, [(i, (i + by) % count) for i in range(count)])


def swap(block, axis):
    return shift(block, axis, 1)


def on_device(
    residual_in,
    dh_rest,
    w_query,
    w_key,
    w_value,
    q_raw,
    k_raw,
    v_win,
    cache_k,
    cache_v,
    d_attn,
    s_qk,
    cache_live,
):
    info = jnp.stack(
        [
            lax.axis_index("z"),
            lax.axis_index("xh"),
            lax.axis_index("xl") * 4 + lax.axis_index("y"),
            lax.axis_index("c"),
            CACHE - cache_live[0],
        ]
    ).astype(jnp.int32)
    gain = s_qk.reshape(1, HD)

    sources = [cache_k, cache_v, k_raw, v_win, residual_in, dh_rest, q_raw, d_attn]
    sources = [pltpu.with_memory_space_constraint(array, pltpu.HBM) for array in sources]
    here, resid_t, dh_t, q_own, do_own = pack_rows(info, *sources, gain)
    there = swap(here, "xh")
    up = shift(here, "z", -1)
    down = shift(here, "z", 1)
    pair_wide = swap(w_query, "c")
    there, late_q, late_do = lax.optimization_barrier((there, q_own, do_own))
    pair_q = swap(late_q, "c")
    pair_do = swap(late_do, "c")
    up_there = shift(there, "z", -1)
    down_there = shift(there, "z", 1)
    far = shift(up, "z", -1)
    groups = [[here], [there], [up], [down]]
    narrow = [w_key.T, w_value.T]
    narrow, pair_do, pair_wide = lax.optimization_barrier((narrow, pair_do, pair_wide))
    pair_weights = [pair_wide] + [swap(w, "c") for w in narrow]
    query, dout, *state = stats_call(
        0, info, groups[:4], [q_own, do_own, pair_q, pair_do, gain]
    )
    far_there = shift(down_there, "z", 1)
    groups += [[up_there], [down_there], [far], [far_there]]
    state = stats_call(4, info, groups[4:6], [query, dout, *state])
    wins = [group[-1] for group in groups[:6]]
    stat, win_k, win_v = stats_call(
        6, info, groups[6:], wins + [query, dout, *state], last=True
    )
    weights = [pltpu.with_memory_space_constraint(w_query, pltpu.HBM), *narrow]
    pair_stat, pair_weights = lax.optimization_barrier((swap(stat, "c"), pair_weights))
    lse, delta, dq, *parts = window_call(info, stat, pair_stat, query, dout, win_k, win_v)
    parts = [parts[0]] + [shift(parts[dz], "z", dz) for dz in (1, 3, 2)]
    dq, w_own, w_kv = cache_call(
        0, info, groups[:5], query, dout, lse, delta, dq, [*weights, *pair_weights]
    )
    parts, dq = lax.optimization_barrier((parts, dq))
    keep, send = sum_parts(info, parts)
    other = swap(send, "xh")
    (dq,) = cache_call(5, info, groups[5:], query, dout, lse, delta, dq)
    other, dq = lax.optimization_barrier((other, dq))
    pair_dq = swap(dq, "c")
    kv = own_kv(info, keep, other, k_raw, gain)
    pair_kv = swap(kv, "c")
    partial = project(info, dq, pair_dq, q_own, pair_q, gain, kv, pair_kv, w_own, w_kv)
    pieces = lax.all_to_all(partial, CHIP_AXES, 0, 0)
    grad_t, sums = row_sums(pieces, resid_t, dh_t)
    everyone = lax.all_to_all(
        jnp.broadcast_to(sums[None], (2 * CHIPS, 8, TOK)), TP_AXES, 0, 0
    )
    return last_norm(grad_t, everyone, resid_t)


def solution(mesh):
    fine = Mesh(mesh.devices.reshape(4, 2, 2, 4, 2), ("z", "xh", "xl", "y", "c"))
    both = P(CTX_AXES, TP_AXES)
    cols = P(None, TP_AXES)
    rows = P(CTX_AXES, None)
    return jax.shard_map(
        on_device,
        mesh=fine,
        in_specs=(both, both, cols, cols, cols, both, rows, rows, rows, rows, both, P(), P()),
        out_specs=both,
        check_vma=False,
    )
```

```python
import functools
import math

import jax
import jax.numpy as jnp
from jax import lax
from jax.experimental import pallas as pl
from jax.experimental.pallas import tpu as pltpu
from jax.sharding import Mesh
from jax.sharding import PartitionSpec as P

D = 8192
KVH = 8
HD = 128
CACHE = 8192
TOKENS = 1024
CTX = 8
TOK = TOKENS // CTX
HEADS = 4
ROWS = 2 * HEADS * TOK
COLS = HEADS * HD
SIDE = HD // 2
CHIPS = 8
FEAT = D // 16
HALF_CACHE = CACHE // CTX // 2
HALF_WIN = TOK // 2
HALF = HALF_CACHE + HALF_WIN
KB = 512
CHUNK = 512
CHUNKS = ROWS // CHUNK
EPS = 1e-06
SCALE = math.sqrt(HD)
EXP_SCALE = SCALE * math.log2(math.e)
NEG = -1e30
VMEM_LIMIT = 24 * 1024 * 1024
TP_AXES = ("xl", "y", "c")
CTX_AXES = ("z", "xh")
CHIP_AXES = ("xl", "y")


HOPS = ((0, 0), (0, 1), (1, 0), (3, 0), (1, 1), (3, 1), (2, 0), (2, 1))
Z, XH, CHIP, CORE, FLOOR = range(5)
SHAPE = jax.ShapeDtypeStruct
STATE = [SHAPE((ROWS, HD), jnp.float32)] * 3
VM = pl.BlockSpec(memory_space=pltpu.VMEM)
SM = pl.BlockSpec(memory_space=pltpu.SMEM)
HB = pl.BlockSpec(memory_space=pltpu.HBM)
SMALL = pltpu.CompilerParams(vmem_limit_bytes=8 * 1024 * 1024)


def contract_last(left, right):
    return lax.dot_general(
        left, right, (((1,), (1,)), ((), ())), preferred_element_type=jnp.float32
    )


def contract_first(left, right):
    return lax.dot_general(
        left, right, (((0,), (0,)), ((), ())), preferred_element_type=jnp.float32
    )


def unit_rows(values, qk_gain):
    width = values.shape[-1]
    mean_sq = jnp.mean(values * values, axis=-1, keepdims=True)
    return values * (lax.rsqrt(mean_sq + EPS) / math.sqrt(width)) * qk_gain


def unit_back(values, qk_gain, grad):
    width = values.shape[-1]
    mean_sq = jnp.mean(values * values, axis=-1, keepdims=True)
    factor = lax.rsqrt(mean_sq + EPS) / math.sqrt(width)
    weighted = qk_gain * grad
    inner = jnp.sum(weighted * values, axis=-1, keepdims=True)
    return factor * (weighted - values * inner / (width * (mean_sq + EPS)))


def head_cols(h):
    return slice(h * HD, (h + 1) * HD)


def head_rows(h):
    return slice(h * TOK, (h + 1) * TOK)


def pack_kernel(
    info_ref,
    ck_ref,
    cv_ref,
    kr_ref,
    vw_ref,
    resid_ref,
    dh_ref,
    q_ref,
    do_ref,
    gain_ref,
    out_ref,
    resid_out,
    dh_out,
    q_out,
    do_out,
    gain_out,
    ck_s,
    kr_s,
    resid_s,
    dh_s,
    sems,
):
    cols = pl.ds(pl.multiple_of(info_ref[CHIP] * HD, HD), HD)
    cache = pl.ds(pl.multiple_of(info_ref[CORE] * HALF_CACHE, HALF_CACHE), HALF_CACHE)
    win = pl.ds(pl.multiple_of(info_ref[CORE] * HALF_WIN, HALF_WIN), HALF_WIN)
    right = pl.ds(HD, HD)
    copies = [
        pltpu.make_async_copy(ck_ref.at[cache, cols], ck_s, sems.at[0]),
        pltpu.make_async_copy(kr_ref.at[win, cols], kr_s, sems.at[1]),
        pltpu.make_async_copy(
            cv_ref.at[cache, cols], out_ref.at[pl.ds(0, HALF_CACHE), right], sems.at[2]
        ),
        pltpu.make_async_copy(
            vw_ref.at[win, cols], out_ref.at[pl.ds(HALF_CACHE, HALF_WIN), right], sems.at[3]
        ),
        pltpu.make_async_copy(resid_ref, resid_s, sems.at[4]),
        pltpu.make_async_copy(dh_ref, dh_s, sems.at[5]),
        pltpu.make_async_copy(q_ref, q_out, sems.at[6]),
        pltpu.make_async_copy(do_ref, do_out, sems.at[7]),
        pltpu.make_async_copy(gain_ref, gain_out, sems.at[8]),
    ]
    for copy in copies:
        copy.start()
    copies[8].wait()
    gain = gain_out[...]
    copies[0].wait()
    out_ref[:HALF_CACHE, :HD] = unit_rows(ck_s[...].astype(jnp.float32), gain).astype(jnp.bfloat16)
    copies[1].wait()
    out_ref[HALF_CACHE:, :HD] = unit_rows(kr_s[...].astype(jnp.float32), gain).astype(jnp.bfloat16)
    copies[2].wait()
    copies[3].wait()
    copies[4].wait()
    resid_out[...] = resid_s[...].astype(jnp.float32).T.astype(jnp.bfloat16)
    copies[5].wait()
    dh_out[...] = dh_s[...].astype(jnp.float32).T.astype(jnp.bfloat16)
    copies[6].wait()
    copies[7].wait()


def pack_rows(info, *operands):
    return pl.pallas_call(
        pack_kernel,
        out_shape=[
            SHAPE((HALF, 2 * HD), jnp.bfloat16),
            SHAPE((FEAT, TOK), jnp.bfloat16),
            SHAPE((FEAT, TOK), jnp.bfloat16),
            SHAPE((TOK, COLS), jnp.bfloat16),
            SHAPE((TOK, COLS), jnp.bfloat16),
            SHAPE((1, HD), jnp.float32),
        ],
        in_specs=[SM] + [HB] * 9,
        out_specs=[VM] * 6,
        scratch_shapes=[
            pltpu.VMEM((HALF_CACHE, HD), jnp.bfloat16),
            pltpu.VMEM((HALF_WIN, HD), jnp.bfloat16),
            pltpu.VMEM((TOK, FEAT), jnp.bfloat16),
            pltpu.VMEM((TOK, FEAT), jnp.bfloat16),
            pltpu.SemaphoreType.DMA((9,)),
        ],
        compiler_params=SMALL,
        name="pack_rows",
    )(info, *operands)


def cost(flops, exps, moved):
    return pl.CostEstimate(
        flops=int(flops), transcendentals=int(exps), bytes_accessed=int(moved)
    )


def block_cost(blocks, dots):
    return cost(
        blocks * dots * 2 * ROWS * KB * HD, blocks * ROWS * KB, blocks * 4 * KB * HD + 2 ** 21
    )


def source(info_ref, dz, dx):
    return lax.bitwise_and(info_ref[Z] + dz, 3) * 2 + lax.bitwise_and(info_ref[XH] + dx, 1)


def source_at(info_ref, n):
    dz = jnp.where(n >= 6, 2, jnp.where(n < 2, 0, jnp.where(lax.bitwise_and(n, 1) == 0, 1, 3)))
    dx = jnp.where(n >= 6, n - 6, jnp.where(n < 2, n, jnp.where(n >= 4, 1, 0)))
    return source(info_ref, dz, dx)


def cache_mask(info_ref, start):
    return start + lax.broadcasted_iota(jnp.int32, (CHUNK, KB), 1) >= info_ref[FLOOR]


def window_mask(info_ref):
    local = lax.broadcasted_iota(jnp.int32, (CHUNK, KB), 1)
    key = (
        lax.shift_right_logical(local, 6) * TOK
        + info_ref[CORE] * HALF_WIN
        + lax.bitwise_and(local, jnp.int32(HALF_WIN - 1))
    )
    token = source(info_ref, 0, 0) * TOK + lax.bitwise_and(
        lax.broadcasted_iota(jnp.int32, (CHUNK, KB), 0), jnp.int32(TOK - 1)
    )
    return key <= token


def chunk(r):
    return slice(r * CHUNK, (r + 1) * CHUNK)


def keys_at(n):
    return pl.ds(pl.multiple_of(n * KB, KB), KB)


def place_cache(pieces, k_s, v_s, at=0):
    for n, group in enumerate(pieces):
        row = (at + n) * KB
        for piece in group:
            rows = min(piece.shape[0], (at + n + 1) * KB - row)
            k_s[row : row + rows, :] = piece[:rows, :HD]
            v_s[row : row + rows, :] = piece[:rows, HD:]
            row += rows


def stat_block(scores, dprobs, mask, rows, m_s, l_s, w_s):
    if mask is not None:
        scores = jnp.where(mask, scores, NEG)
    old = m_s[rows, :]
    top = old
    for g in range(KB // HD):
        top = jnp.maximum(top, scores[:, head_cols(g)])
    keep = jnp.exp2((old - top) * EXP_SCALE)
    total = l_s[rows, :] * keep
    weighted = w_s[rows, :] * keep
    for g in range(KB // HD):
        e = jnp.exp2((scores[:, head_cols(g)] - top) * EXP_SCALE)
        if mask is not None:
            e = jnp.where(mask[:, head_cols(g)], e, 0.0)
        total = total + e
        weighted = weighted + e * dprobs[:, head_cols(g)]
    m_s[rows, :] = top
    l_s[rows, :] = total
    w_s[rows, :] = weighted


def cache_loop(info_ref, first, count, core, body):
    @pl.loop(0, count)
    def _(n):
        start = source_at(info_ref, first + n) * (2 * KB) + core * KB

        @pl.when((start + KB > info_ref[FLOOR]) & (start < info_ref[FLOOR]))
        def _():
            body(n, start, True)

        @pl.when(start >= info_ref[FLOOR])
        def _():
            body(n, start, False)


def pipelined(dots, rest):
    ready = dots(0)
    for r in range(CHUNKS):
        following = dots(r + 1) if r + 1 < CHUNKS else None
        rest(r, *ready)
        ready = following


def stats_kernel(first, groups, last, info_ref, *refs):
    refs = list(refs)
    flat = [refs.pop(0) for _ in range(sum(groups))]
    pieces = []
    for size in groups:
        pieces.append([flat.pop(0) for _ in range(size)])
    core = info_ref[CORE]
    if first == 0:
        q_ref, do_ref, pair_q_ref, pair_do_ref, gain_ref = refs[:5]
        q_s, do_s, m_s, l_s, w_s = refs[5:10]
        scratch = refs[10:]
        gain = gain_ref[...]
        for side, (raw_ref, grad_ref) in enumerate(((q_ref, do_ref), (pair_q_ref, pair_do_ref))):
            for h in range(HEADS):
                rows = slice((side * HEADS + h) * TOK, (side * HEADS + h + 1) * TOK)
                raw = raw_ref[:, head_cols(h)].astype(jnp.float32)
                q_s[rows, :] = unit_rows(raw, gain).astype(jnp.bfloat16)
                do_s[rows, :] = grad_ref[:, head_cols(h)]
        m_s[...] = jnp.full((ROWS, HD), NEG, jnp.float32)
        l_s[...] = jnp.zeros((ROWS, HD), jnp.float32)
        w_s[...] = jnp.zeros((ROWS, HD), jnp.float32)
    else:
        wins = []
        if last:
            wins = [refs.pop(0) for _ in range(first)]
        q_s, do_s, m_in, l_in, w_in = refs[:5]
        if last:
            stat_ref, wk_ref, wv_ref = refs[5:8]
            m_s, l_s, w_s = refs[8:11]
            scratch = refs[11:]
        else:
            m_s, l_s, w_s = refs[5:8]
            scratch = refs[8:]
        m_s[...] = m_in[...]
        l_s[...] = l_in[...]
        w_s[...] = w_in[...]
    k_s, v_s = scratch
    place_cache(pieces, k_s, v_s)

    def body(n, start, masked):
        keys = k_s[keys_at(n), :]
        values = v_s[keys_at(n), :]
        mask = cache_mask(info_ref, start) if masked else None

        def dots(r):
            return (
                contract_last(q_s[chunk(r), :], keys),
                contract_last(do_s[chunk(r), :], values),
            )

        def rest(r, scores, dprobs):
            stat_block(scores, dprobs, mask, chunk(r), m_s, l_s, w_s)

        pipelined(dots, rest)

    cache_loop(info_ref, first, len(groups), core, body)
    if last:
        for n, piece in enumerate(wins + [group[-1] for group in pieces]):
            at = pl.multiple_of(source(info_ref, *HOPS[n]) * HALF_WIN, HALF_WIN)
            low = piece.shape[0] - HALF_WIN
            wk_ref[pl.ds(at, HALF_WIN), :] = piece[low:, :HD]
            wv_ref[pl.ds(at, HALF_WIN), :] = piece[low:, HD:]

        win_mask = window_mask(info_ref)
        win_keys = wk_ref[...]
        win_values = wv_ref[...]

        def win_dots(r):
            return (
                contract_last(q_s[chunk(r), :], win_keys),
                contract_last(do_s[chunk(r), :], win_values),
            )

        def win_rest(r, scores, dprobs):
            stat_block(scores, dprobs, win_mask, chunk(r), m_s, l_s, w_s)

        pipelined(win_dots, win_rest)

        top = jnp.max(m_s[...], axis=1, keepdims=True)
        fix = jnp.exp2((m_s[...] - top) * EXP_SCALE)
        total = jnp.sum(l_s[...] * fix, axis=1, keepdims=True)
        weighted = jnp.sum(w_s[...] * fix, axis=1, keepdims=True)
        lane = lax.broadcasted_iota(jnp.int32, (ROWS, HD), 1)
        stat_ref[...] = jnp.where(lane == 0, top, jnp.where(lane == 1, total, weighted))


def stats_call(first, info, groups, rest, last=False):
    pieces = [piece for group in groups for piece in group]
    if first == 0:
        out = [SHAPE((ROWS, HD), jnp.bfloat16)] * 2 + STATE
    elif last:
        out = [SHAPE((ROWS, HD), jnp.float32)] + [SHAPE((KB, HD), jnp.bfloat16)] * 2
    else:
        out = STATE
    keys = len(groups) * KB
    scratch = [pltpu.VMEM((keys, HD), jnp.bfloat16)] * 2
    if last:
        scratch = [pltpu.VMEM((ROWS, HD), jnp.float32)] * 3 + scratch
    return pl.pallas_call(
        functools.partial(stats_kernel, first, [len(group) for group in groups], last),
        out_shape=out,
        in_specs=[SM] + [VM] * (len(pieces) + len(rest)),
        out_specs=[VM] * len(out),
        scratch_shapes=scratch,
        compiler_params=pltpu.CompilerParams(vmem_limit_bytes=VMEM_LIMIT),
        cost_estimate=block_cost(len(groups) + (1 if last else 0), 2),
        name="stats_" + str(first),
    )(info, *pieces, *rest)


def grad_block(scores, dprobs, mask, lse, delta):
    probs = []
    dscores = []
    for g in range(KB // HD):
        p = jnp.exp2(scores[:, head_cols(g)] * EXP_SCALE - lse)
        if mask is not None:
            p = jnp.where(mask[:, head_cols(g)], p, 0.0)
        probs.append(p.astype(jnp.bfloat16))
        dscores.append((p * (dprobs[:, head_cols(g)] - delta)).astype(jnp.bfloat16))
    return jnp.concatenate(probs, 1), jnp.concatenate(dscores, 1)


def window_kernel(
    info_ref, mine_ref, pair_ref, q_s, do_s, wk_ref, wv_ref, lse_ref, delta_ref, dq_ref, *rest
):
    parts, dkv_ref = rest[:4], rest[4]
    mine = mine_ref[...]
    half = ROWS // 2
    pair = jnp.concatenate([pair_ref[half:, :], pair_ref[:half, :]], 0)
    top = jnp.maximum(mine[:, 0:1], pair[:, 0:1])
    fix = jnp.exp2((mine[:, 0:1] - top) * EXP_SCALE)
    pair_fix = jnp.exp2((pair[:, 0:1] - top) * EXP_SCALE)
    total = mine[:, 1:2] * fix + pair[:, 1:2] * pair_fix
    weighted = mine[:, 2:3] * fix + pair[:, 2:3] * pair_fix
    lse_ref[...] = jnp.broadcast_to(top * EXP_SCALE + jnp.log2(total), (ROWS, HD))
    delta_ref[...] = jnp.broadcast_to(weighted / total, (ROWS, HD))
    dkv_ref[...] = jnp.zeros((KB, 2 * HD), jnp.float32)

    mask = window_mask(info_ref)
    keys = wk_ref[...]
    values = wv_ref[...]

    def dots(r):
        return contract_last(q_s[chunk(r), :], keys), contract_last(do_s[chunk(r), :], values)

    def rest(r, scores, dprobs):
        rows = chunk(r)
        probs, dscores = grad_block(scores, dprobs, mask, lse_ref[rows, :], delta_ref[rows, :])
        dq_ref[rows, :] = jnp.dot(dscores, keys, preferred_element_type=jnp.float32)
        dkv_ref[:, :HD] += contract_first(dscores, q_s[rows, :])
        dkv_ref[:, HD:] += contract_first(probs, do_s[rows, :])

    pipelined(dots, rest)

    for dz in range(4):
        at = pl.multiple_of(lax.bitwise_and(info_ref[Z] + dz, 3) * TOK, TOK)
        parts[dz][...] = dkv_ref[pl.ds(at, TOK), :]


def window_call(info, mine, pair, query, dout, win_k, win_v):
    out = STATE + [SHAPE((TOK, 2 * HD), jnp.float32)] * 4
    return pl.pallas_call(
        window_kernel,
        out_shape=out,
        in_specs=[SM] + [VM] * 6,
        out_specs=[VM] * 7,
        scratch_shapes=[pltpu.VMEM((KB, 2 * HD), jnp.float32)],
        compiler_params=pltpu.CompilerParams(vmem_limit_bytes=VMEM_LIMIT),
        cost_estimate=block_cost(1, 5),
        name="window_grads",
    )(info, mine, pair, query, dout, win_k, win_v)


def fetches(info_ref, weights, w_ref, kv_ref, sems):
    wq_ref, wk_ref, wv_ref, pair_wq_ref, pair_wk_ref, pair_wv_ref = weights
    copies = []
    for j in range(CHIPS):
        rows = pl.ds(pl.multiple_of((2 * j + info_ref[CORE]) * FEAT, FEAT), FEAT)
        for n, ref in enumerate((wq_ref, pair_wq_ref)):
            target = w_ref.at[j, :, pl.ds(n * COLS, COLS)]
            copies.append(pltpu.make_async_copy(ref.at[rows, :], target, sems.at[j, n]))
        for n, ref in enumerate((wk_ref, wv_ref, pair_wk_ref, pair_wv_ref)):
            target = kv_ref.at[j, pl.ds(n * SIDE, SIDE), :]
            copies.append(pltpu.make_async_copy(ref.at[:, rows], target, sems.at[j, 2 + n]))
    return copies


def cache_kernel(first, groups, info_ref, *refs):
    refs = list(refs)
    copies = []
    if first == 0:
        sems = refs.pop()
        weights = [refs.pop(0) for _ in range(6)]
        w_ref, kv_ref = refs[-4], refs[-3]
        del refs[-4:-2]
        copies = fetches(info_ref, weights, w_ref, kv_ref, sems)
    for copy in copies:
        copy.start()
    pieces = []
    for size in groups:
        pieces.append([refs.pop(0) for _ in range(size)])
    q_s, do_s, lse_ref, delta_ref, dq_in, dq_ref, k_s, v_s = refs
    place_cache(pieces, k_s, v_s)
    dq_ref[...] = dq_in[...]

    def body(n, start, masked):
        keys = k_s[keys_at(n), :]
        values = v_s[keys_at(n), :]
        mask = cache_mask(info_ref, start) if masked else None

        def dots(r):
            return contract_last(q_s[chunk(r), :], keys), contract_last(do_s[chunk(r), :], values)

        def rest(r, scores, dprobs):
            rows = chunk(r)
            _, dscores = grad_block(scores, dprobs, mask, lse_ref[rows, :], delta_ref[rows, :])
            dq_ref[rows, :] += jnp.dot(dscores, keys, preferred_element_type=jnp.float32)

        pipelined(dots, rest)

    cache_loop(info_ref, first, len(groups), info_ref[CORE], body)
    for copy in copies:
        copy.wait()


def cache_call(first, info, groups, query, dout, lse, delta, dq, weights=()):
    pieces = [piece for group in groups for piece in group]
    out = STATE[:1]
    scratch = [pltpu.VMEM((len(groups) * KB, HD), jnp.bfloat16)] * 2
    if weights:
        out = out + [
            SHAPE((CHIPS, FEAT, 2 * COLS), jnp.bfloat16),
            SHAPE((CHIPS, 2 * HD, FEAT), jnp.bfloat16),
        ]
        scratch = scratch + [pltpu.SemaphoreType.DMA((CHIPS, 6))]
    return pl.pallas_call(
        functools.partial(cache_kernel, first, [len(group) for group in groups]),
        out_shape=out,
        in_specs=[SM] + [HB] * len(weights) + [VM] * (len(pieces) + 5),
        out_specs=[VM] * len(out),
        scratch_shapes=scratch,
        compiler_params=pltpu.CompilerParams(vmem_limit_bytes=VMEM_LIMIT),
        cost_estimate=block_cost(len(groups), 3),
        name="cache_grads_" + str(first),
    )(info, *weights, *pieces, query, dout, lse, delta, dq)


def sum_kernel(info_ref, a_ref, b_ref, c_ref, d_ref, keep_ref, send_ref):
    total = (a_ref[...] + b_ref[...]) + (c_ref[...] + d_ref[...])
    first = info_ref[XH] == 0
    keep_ref[...] = jnp.where(first, total[:HALF_WIN, :], total[HALF_WIN:, :])
    send_ref[...] = jnp.where(first, total[HALF_WIN:, :], total[:HALF_WIN, :])


def sum_parts(info, parts):
    return pl.pallas_call(
        sum_kernel,
        out_shape=[SHAPE((HALF_WIN, 2 * HD), jnp.float32)] * 2,
        in_specs=[SM] + [VM] * 4,
        out_specs=[VM] * 2,
        compiler_params=SMALL,
        name="sum_parts",
    )(info, *parts)


def own_kv_kernel(idx_ref, keep_ref, other_ref, raw_ref, gain_ref, out_ref):
    total = keep_ref[...] + other_ref[...]
    raw = raw_ref[...].astype(jnp.float32)
    out_ref[:, :HD] = unit_back(raw, gain_ref[...], total[:, :HD] * SCALE).astype(jnp.bfloat16)
    out_ref[:, HD:] = total[:, HD:].astype(jnp.bfloat16)


def own_kv(idx, keep, other, k_raw, gain):
    def whole(i, idx):
        return (0, 0)

    return pl.pallas_call(
        own_kv_kernel,
        out_shape=SHAPE((HALF_WIN, 2 * HD), jnp.bfloat16),
        grid_spec=pltpu.PrefetchScalarGridSpec(
            num_scalar_prefetch=1,
            grid=(1,),
            in_specs=[
                pl.BlockSpec((HALF_WIN, 2 * HD), whole),
                pl.BlockSpec((HALF_WIN, 2 * HD), whole),
                pl.BlockSpec((HALF_WIN, HD), lambda i, idx: (idx[CORE], idx[CHIP])),
                pl.BlockSpec((1, HD), whole),
            ],
            out_specs=pl.BlockSpec((HALF_WIN, 2 * HD), whole),
        ),
        compiler_params=SMALL,
        name="own_kv",
    )(idx, keep, other, k_raw, gain)


def project_kernel(
    info_ref,
    dq_ref,
    pair_dq_ref,
    q_ref,
    pair_q_ref,
    gain_ref,
    kv_ref,
    pair_kv_ref,
    w_ref,
    wkv_ref,
    out_ref,
    g_s,
):
    core = info_ref[CORE]
    gain = gain_ref[...]
    for h in range(HEADS):
        rows = head_rows(h)
        low = slice(ROWS // 2 + h * TOK, ROWS // 2 + (h + 1) * TOK)
        for side, raw_ref, grad in (
            (0, q_ref, dq_ref[rows, :] + pair_dq_ref[low, :]),
            (1, pair_q_ref, dq_ref[low, :] + pair_dq_ref[rows, :]),
        ):
            raw = raw_ref[:, head_cols(h)].astype(jnp.float32)
            at = side * COLS + h * HD
            g_s[at : at + HD, :] = unit_back(raw, gain, grad * SCALE).T.astype(jnp.bfloat16)
    here = kv_ref[...].astype(jnp.float32)
    there = pair_kv_ref[...].astype(jnp.float32)
    top = jnp.where(core == 0, here, there)
    bottom = jnp.where(core == 0, there, here)
    kv = jnp.concatenate([top, bottom], 0)
    for n in range(2):
        both = kv[:, n * HD : (n + 1) * HD].T.astype(jnp.bfloat16)
        first = jnp.where(core == 0, both[:SIDE, :], both[SIDE:, :])
        second = jnp.where(core == 0, both[SIDE:, :], both[:SIDE, :])
        g_s[2 * COLS + n * SIDE : 2 * COLS + (n + 1) * SIDE, :] = first
        g_s[2 * COLS + (2 + n) * SIDE : 2 * COLS + (3 + n) * SIDE, :] = second
    for j in range(CHIPS):
        total = contract_first(wkv_ref[j], g_s[2 * COLS :, :])
        total += jnp.dot(w_ref[j], g_s[: 2 * COLS, :], preferred_element_type=jnp.float32)
        out_ref[j] = total.astype(jnp.bfloat16)


def project(info, *operands):
    return pl.pallas_call(
        project_kernel,
        out_shape=SHAPE((CHIPS, FEAT, TOK), jnp.bfloat16),
        in_specs=[SM] + [VM] * 9,
        out_specs=VM,
        scratch_shapes=[pltpu.VMEM((2 * COLS + 2 * HD, TOK), jnp.bfloat16)],
        compiler_params=pltpu.CompilerParams(vmem_limit_bytes=VMEM_LIMIT),
        cost_estimate=cost(2 * TOK * D // 2 * 1280, 0, 12e6),
        name="project",
    )(info, *operands)


def rows_kernel(pieces_ref, resid_ref, dh_ref, grad_ref, sums_ref):
    inner = jnp.zeros((1, TOK), jnp.float32)
    square = jnp.zeros((1, TOK), jnp.float32)
    for n in range(FEAT // HD):
        rows = head_cols(n)
        grad = pieces_ref[0, rows, :].astype(jnp.float32)
        for m in range(1, CHIPS):
            grad += pieces_ref[m, rows, :].astype(jnp.float32)
        grad += dh_ref[rows, :].astype(jnp.float32)
        grad_ref[rows, :] = grad
        resid = resid_ref[rows, :].astype(jnp.float32)
        inner += jnp.sum(grad * resid, axis=0, keepdims=True)
        square += jnp.sum(resid * resid, axis=0, keepdims=True)
    row = lax.broadcasted_iota(jnp.int32, (8, TOK), 0)
    sums_ref[...] = jnp.where(row == 0, inner, square)


def row_sums(pieces, resid_t, dh_t):
    return pl.pallas_call(
        rows_kernel,
        out_shape=[SHAPE((FEAT, TOK), jnp.float32), SHAPE((8, TOK), jnp.float32)],
        in_specs=[VM] * 3,
        out_specs=[VM] * 2,
        compiler_params=SMALL,
        name="row_sums",
    )(pieces, resid_t, dh_t)


def norm_kernel(grad_ref, sums_ref, resid_ref, out_ref):
    sums = sums_ref[0]
    for n in range(1, 2 * CHIPS):
        sums += sums_ref[n]
    mean_sq = sums[1:2, :] / D
    factor = lax.rsqrt(mean_sq + EPS) / math.sqrt(D)
    correction = sums[0:1, :] / (D * (mean_sq + EPS))
    for n in range(FEAT // HD):
        rows = head_cols(n)
        resid = resid_ref[rows, :].astype(jnp.float32)
        out_ref[:, rows] = (factor * (grad_ref[rows, :] - resid * correction)).T


def last_norm(grad_t, sums, resid_t):
    return pl.pallas_call(
        norm_kernel,
        out_shape=SHAPE((TOK, FEAT), jnp.float32),
        in_specs=[VM] * 3,
        out_specs=VM,
        compiler_params=SMALL,
        name="last_norm",
    )(grad_t, sums, resid_t)


def shift(block, axis, by):
    count = lax.axis_size(axis)
    return lax.ppermute(block, axis, [(i, (i + by) % count) for i in range(count)])


def swap(block, axis):
    return shift(block, axis, 1)


def on_device(
    residual_in,
    dh_rest,
    w_query,
    w_key,
    w_value,
    q_raw,
    k_raw,
    v_win,
    cache_k,
    cache_v,
    d_attn,
    s_qk,
    cache_live,
):
    info = jnp.stack(
        [
            lax.axis_index("z"),
            lax.axis_index("xh"),
            lax.axis_index("xl") * 4 + lax.axis_index("y"),
            lax.axis_index("c"),
            CACHE - cache_live[0],
        ]
    ).astype(jnp.int32)
    sources = [cache_k, cache_v, k_raw, v_win, residual_in, dh_rest, q_raw, d_attn]
    sources.append(s_qk.reshape(1, HD))
    sources = [pltpu.with_memory_space_constraint(array, pltpu.HBM) for array in sources]
    here, resid_t, dh_t, q_own, do_own, gain = pack_rows(info, *sources)
    there = swap(here, "xh")
    up = shift(here, "z", -1)
    down = shift(here, "z", 1)
    pair_wide = swap(w_query, "c")
    there, late_q, late_do = lax.optimization_barrier((there, q_own, do_own))
    pair_q = swap(late_q, "c")
    pair_do = swap(late_do, "c")
    up_there = shift(there, "z", -1)
    down_there = shift(there, "z", 1)
    far = shift(up, "z", -1)
    groups = [[here], [there], [up], [down]]
    narrow = [w_key.T, w_value.T]
    narrow, pair_do, pair_wide = lax.optimization_barrier((narrow, pair_do, pair_wide))
    pair_weights = [pair_wide] + [swap(w, "c") for w in narrow]
    query, dout, *state = stats_call(
        0, info, groups[:4], [q_own, do_own, pair_q, pair_do, gain]
    )
    far_there = shift(down_there, "z", 1)
    groups += [[up_there], [down_there], [far], [far_there]]
    state = stats_call(4, info, groups[4:6], [query, dout, *state])
    wins = [group[-1] for group in groups[:6]]
    stat, win_k, win_v = stats_call(
        6, info, groups[6:], wins + [query, dout, *state], last=True
    )
    weights = [pltpu.with_memory_space_constraint(w_query, pltpu.HBM), *narrow]
    pair_stat, pair_weights = lax.optimization_barrier((swap(stat, "c"), pair_weights))
    lse, delta, dq, *parts = window_call(info, stat, pair_stat, query, dout, win_k, win_v)
    parts = [parts[0]] + [shift(parts[dz], "z", dz) for dz in (1, 3, 2)]
    dq, w_own, w_kv = cache_call(
        0, info, groups[:5], query, dout, lse, delta, dq, [*weights, *pair_weights]
    )
    parts, dq = lax.optimization_barrier((parts, dq))
    keep, send = sum_parts(info, parts)
    other = swap(send, "xh")
    (dq,) = cache_call(5, info, groups[5:], query, dout, lse, delta, dq)
    other, dq = lax.optimization_barrier((other, dq))
    pair_dq = swap(dq, "c")
    kv = own_kv(info, keep, other, k_raw, gain)
    pair_kv = swap(kv, "c")
    partial = project(info, dq, pair_dq, q_own, pair_q, gain, kv, pair_kv, w_own, w_kv)
    pieces = lax.all_to_all(partial, CHIP_AXES, 0, 0)
    grad_t, sums = row_sums(pieces, resid_t, dh_t)
    everyone = lax.all_to_all(
        jnp.broadcast_to(sums[None], (2 * CHIPS, 8, TOK)), TP_AXES, 0, 0
    )
    return last_norm(grad_t, everyone, resid_t)


def solution(mesh):
    fine = Mesh(mesh.devices.reshape(4, 2, 2, 4, 2), ("z", "xh", "xl", "y", "c"))
    both = P(CTX_AXES, TP_AXES)
    cols = P(None, TP_AXES)
    rows = P(CTX_AXES, None)
    return jax.shard_map(
        on_device,
        mesh=fine,
        in_specs=(both, both, cols, cols, cols, both, rows, rows, rows, rows, both, P(), P()),
        out_specs=both,
        check_vma=False,
    )
```

```python
import functools
import math

import jax
import jax.numpy as jnp
from jax import lax
from jax.experimental import pallas as pl
from jax.experimental.pallas import tpu as pltpu
from jax.sharding import Mesh
from jax.sharding import PartitionSpec as P

D = 8192
KVH = 8
HD = 128
CACHE = 8192
TOKENS = 1024
CTX = 8
TOK = TOKENS // CTX
HEADS = 4
ROWS = 2 * HEADS * TOK
COLS = HEADS * HD
SIDE = HD // 2
CHIPS = 8
FEAT = D // 16
HALF_CACHE = CACHE // CTX // 2
HALF_WIN = TOK // 2
HALF = HALF_CACHE + HALF_WIN
KB = 512
CHUNK = 512
CHUNKS = ROWS // CHUNK
EPS = 1e-06
SCALE = math.sqrt(HD)
EXP_SCALE = SCALE * math.log2(math.e)
NEG = -1e30
VMEM_LIMIT = 24 * 1024 * 1024
TP_AXES = ("xl", "y", "c")
CTX_AXES = ("z", "xh")
CHIP_AXES = ("xl", "y")


HOPS = ((0, 0), (0, 1), (1, 0), (3, 0), (1, 1), (3, 1), (2, 0), (2, 1))
Z, XH, CHIP, CORE, FLOOR = range(5)
SHAPE = jax.ShapeDtypeStruct
STATE = [SHAPE((ROWS, HD), jnp.float32)] * 3
VM = pl.BlockSpec(memory_space=pltpu.VMEM)
SM = pl.BlockSpec(memory_space=pltpu.SMEM)
HB = pl.BlockSpec(memory_space=pltpu.HBM)
SMALL = pltpu.CompilerParams(vmem_limit_bytes=8 * 1024 * 1024)


def contract_last(left, right):
    return lax.dot_general(
        left, right, (((1,), (1,)), ((), ())), preferred_element_type=jnp.float32
    )


def contract_first(left, right):
    return lax.dot_general(
        left, right, (((0,), (0,)), ((), ())), preferred_element_type=jnp.float32
    )


def unit_rows(values, qk_gain):
    width = values.shape[-1]
    mean_sq = jnp.mean(values * values, axis=-1, keepdims=True)
    return values * (lax.rsqrt(mean_sq + EPS) / math.sqrt(width)) * qk_gain


def unit_back(values, qk_gain, grad):
    width = values.shape[-1]
    mean_sq = jnp.mean(values * values, axis=-1, keepdims=True)
    factor = lax.rsqrt(mean_sq + EPS) / math.sqrt(width)
    weighted = qk_gain * grad
    inner = jnp.sum(weighted * values, axis=-1, keepdims=True)
    return factor * (weighted - values * inner / (width * (mean_sq + EPS)))


def head_cols(h):
    return slice(h * HD, (h + 1) * HD)


def head_rows(h):
    return slice(h * TOK, (h + 1) * TOK)


def pack_kernel(
    info_ref,
    ck_ref,
    cv_ref,
    kr_ref,
    vw_ref,
    resid_ref,
    dh_ref,
    q_ref,
    do_ref,
    gain_ref,
    out_ref,
    resid_out,
    dh_out,
    q_out,
    do_out,
    gain_out,
    ck_s,
    kr_s,
    resid_s,
    dh_s,
    sems,
):
    cols = pl.ds(pl.multiple_of(info_ref[CHIP] * HD, HD), HD)
    cache = pl.ds(pl.multiple_of(info_ref[CORE] * HALF_CACHE, HALF_CACHE), HALF_CACHE)
    win = pl.ds(pl.multiple_of(info_ref[CORE] * HALF_WIN, HALF_WIN), HALF_WIN)
    right = pl.ds(HD, HD)
    copies = [
        pltpu.make_async_copy(ck_ref.at[cache, cols], ck_s, sems.at[0]),
        pltpu.make_async_copy(kr_ref.at[win, cols], kr_s, sems.at[1]),
        pltpu.make_async_copy(
            cv_ref.at[cache, cols], out_ref.at[pl.ds(0, HALF_CACHE), right], sems.at[2]
        ),
        pltpu.make_async_copy(
            vw_ref.at[win, cols], out_ref.at[pl.ds(HALF_CACHE, HALF_WIN), right], sems.at[3]
        ),
        pltpu.make_async_copy(resid_ref, resid_s, sems.at[4]),
        pltpu.make_async_copy(dh_ref, dh_s, sems.at[5]),
        pltpu.make_async_copy(q_ref, q_out, sems.at[6]),
        pltpu.make_async_copy(do_ref, do_out, sems.at[7]),
        pltpu.make_async_copy(gain_ref, gain_out, sems.at[8]),
    ]
    for copy in copies:
        copy.start()
    copies[8].wait()
    gain = gain_out[...]
    copies[0].wait()
    out_ref[:HALF_CACHE, :HD] = unit_rows(ck_s[...].astype(jnp.float32), gain).astype(jnp.bfloat16)
    copies[1].wait()
    out_ref[HALF_CACHE:, :HD] = unit_rows(kr_s[...].astype(jnp.float32), gain).astype(jnp.bfloat16)
    copies[2].wait()
    copies[3].wait()
    copies[4].wait()
    resid_out[...] = resid_s[...].astype(jnp.float32).T.astype(jnp.bfloat16)
    copies[5].wait()
    dh_out[...] = dh_s[...].astype(jnp.float32).T.astype(jnp.bfloat16)
    copies[6].wait()
    copies[7].wait()


def pack_rows(info, *operands):
    return pl.pallas_call(
        pack_kernel,
        out_shape=[
            SHAPE((HALF, 2 * HD), jnp.bfloat16),
            SHAPE((FEAT, TOK), jnp.bfloat16),
            SHAPE((FEAT, TOK), jnp.bfloat16),
            SHAPE((TOK, COLS), jnp.bfloat16),
            SHAPE((TOK, COLS), jnp.bfloat16),
            SHAPE((1, HD), jnp.float32),
        ],
        in_specs=[SM] + [HB] * 9,
        out_specs=[VM] * 6,
        scratch_shapes=[
            pltpu.VMEM((HALF_CACHE, HD), jnp.bfloat16),
            pltpu.VMEM((HALF_WIN, HD), jnp.bfloat16),
            pltpu.VMEM((TOK, FEAT), jnp.bfloat16),
            pltpu.VMEM((TOK, FEAT), jnp.bfloat16),
            pltpu.SemaphoreType.DMA((9,)),
        ],
        compiler_params=SMALL,
        name="pack_rows",
    )(info, *operands)


def cost(flops, exps, moved):
    return pl.CostEstimate(
        flops=int(flops), transcendentals=int(exps), bytes_accessed=int(moved)
    )


def block_cost(blocks, dots):
    return cost(
        blocks * dots * 2 * ROWS * KB * HD, blocks * ROWS * KB, blocks * 4 * KB * HD + 2 ** 21
    )


def source(info_ref, dz, dx):
    return lax.bitwise_and(info_ref[Z] + dz, 3) * 2 + lax.bitwise_and(info_ref[XH] + dx, 1)


def source_at(info_ref, n):
    dz = jnp.where(n >= 6, 2, jnp.where(n < 2, 0, jnp.where(lax.bitwise_and(n, 1) == 0, 1, 3)))
    dx = jnp.where(n >= 6, n - 6, jnp.where(n < 2, n, jnp.where(n >= 4, 1, 0)))
    return source(info_ref, dz, dx)


def cache_mask(info_ref, start):
    return start + lax.broadcasted_iota(jnp.int32, (CHUNK, KB), 1) >= info_ref[FLOOR]


def window_mask(info_ref):
    local = lax.broadcasted_iota(jnp.int32, (CHUNK, KB), 1)
    key = (
        lax.shift_right_logical(local, 6) * TOK
        + info_ref[CORE] * HALF_WIN
        + lax.bitwise_and(local, jnp.int32(HALF_WIN - 1))
    )
    token = source(info_ref, 0, 0) * TOK + lax.bitwise_and(
        lax.broadcasted_iota(jnp.int32, (CHUNK, KB), 0), jnp.int32(TOK - 1)
    )
    return key <= token


def chunk(r):
    return slice(r * CHUNK, (r + 1) * CHUNK)


def keys_at(n):
    return pl.ds(pl.multiple_of(n * KB, KB), KB)


def place_cache(pieces, k_s, v_s, at=0):
    for n, group in enumerate(pieces):
        row = (at + n) * KB
        for piece in group:
            rows = min(piece.shape[0], (at + n + 1) * KB - row)
            k_s[row : row + rows, :] = piece[:rows, :HD]
            v_s[row : row + rows, :] = piece[:rows, HD:]
            row += rows


def stat_block(scores, dprobs, mask, rows, m_s, l_s, w_s):
    if mask is not None:
        scores = jnp.where(mask, scores, NEG)
    old = m_s[rows, :]
    top = old
    for g in range(KB // HD):
        top = jnp.maximum(top, scores[:, head_cols(g)])
    keep = jnp.exp2((old - top) * EXP_SCALE)
    total = l_s[rows, :] * keep
    weighted = w_s[rows, :] * keep
    for g in range(KB // HD):
        e = jnp.exp2((scores[:, head_cols(g)] - top) * EXP_SCALE)
        if mask is not None:
            e = jnp.where(mask[:, head_cols(g)], e, 0.0)
        total = total + e
        weighted = weighted + e * dprobs[:, head_cols(g)]
    m_s[rows, :] = top
    l_s[rows, :] = total
    w_s[rows, :] = weighted


def cache_loop(info_ref, first, count, core, body):
    @pl.loop(0, count)
    def _(n):
        start = source_at(info_ref, first + n) * (2 * KB) + core * KB

        @pl.when((start + KB > info_ref[FLOOR]) & (start < info_ref[FLOOR]))
        def _():
            body(n, start, True)

        @pl.when(start >= info_ref[FLOOR])
        def _():
            body(n, start, False)


def pipelined(dots, rest):
    ready = dots(0)
    for r in range(CHUNKS):
        following = dots(r + 1) if r + 1 < CHUNKS else None
        rest(r, *ready)
        ready = following


def stats_kernel(first, groups, last, info_ref, *refs):
    refs = list(refs)
    flat = [refs.pop(0) for _ in range(sum(groups))]
    pieces = []
    for size in groups:
        pieces.append([flat.pop(0) for _ in range(size)])
    core = info_ref[CORE]
    if first == 0:
        q_ref, do_ref, pair_q_ref, pair_do_ref, gain_ref = refs[:5]
        q_s, do_s, m_s, l_s, w_s = refs[5:10]
        scratch = refs[10:]
        gain = gain_ref[...]
        for side, (raw_ref, grad_ref) in enumerate(((q_ref, do_ref), (pair_q_ref, pair_do_ref))):
            for h in range(HEADS):
                rows = slice((side * HEADS + h) * TOK, (side * HEADS + h + 1) * TOK)
                raw = raw_ref[:, head_cols(h)].astype(jnp.float32)
                q_s[rows, :] = unit_rows(raw, gain).astype(jnp.bfloat16)
                do_s[rows, :] = grad_ref[:, head_cols(h)]
        m_s[...] = jnp.full((ROWS, HD), NEG, jnp.float32)
        l_s[...] = jnp.zeros((ROWS, HD), jnp.float32)
        w_s[...] = jnp.zeros((ROWS, HD), jnp.float32)
    else:
        wins = []
        if last:
            wins = [refs.pop(0) for _ in range(first)]
        q_s, do_s, m_in, l_in, w_in = refs[:5]
        if last:
            stat_ref, wk_ref, wv_ref = refs[5:8]
            m_s, l_s, w_s = refs[8:11]
            scratch = refs[11:]
        else:
            m_s, l_s, w_s = refs[5:8]
            scratch = refs[8:]
        m_s[...] = m_in[...]
        l_s[...] = l_in[...]
        w_s[...] = w_in[...]
    k_s, v_s = scratch
    place_cache(pieces, k_s, v_s)

    def body(n, start, masked):
        keys = k_s[keys_at(n), :]
        values = v_s[keys_at(n), :]
        mask = cache_mask(info_ref, start) if masked else None

        def dots(r):
            return (
                contract_last(q_s[chunk(r), :], keys),
                contract_last(do_s[chunk(r), :], values),
            )

        def rest(r, scores, dprobs):
            stat_block(scores, dprobs, mask, chunk(r), m_s, l_s, w_s)

        pipelined(dots, rest)

    cache_loop(info_ref, first, len(groups), core, body)
    if last:
        for n, piece in enumerate(wins + [group[-1] for group in pieces]):
            at = pl.multiple_of(source(info_ref, *HOPS[n]) * HALF_WIN, HALF_WIN)
            low = piece.shape[0] - HALF_WIN
            wk_ref[pl.ds(at, HALF_WIN), :] = piece[low:, :HD]
            wv_ref[pl.ds(at, HALF_WIN), :] = piece[low:, HD:]

        win_mask = window_mask(info_ref)
        win_keys = wk_ref[...]
        win_values = wv_ref[...]

        def win_dots(r):
            return (
                contract_last(q_s[chunk(r), :], win_keys),
                contract_last(do_s[chunk(r), :], win_values),
            )

        def win_rest(r, scores, dprobs):
            stat_block(scores, dprobs, win_mask, chunk(r), m_s, l_s, w_s)

        pipelined(win_dots, win_rest)

        top = jnp.max(m_s[...], axis=1, keepdims=True)
        fix = jnp.exp2((m_s[...] - top) * EXP_SCALE)
        total = jnp.sum(l_s[...] * fix, axis=1, keepdims=True)
        weighted = jnp.sum(w_s[...] * fix, axis=1, keepdims=True)
        lane = lax.broadcasted_iota(jnp.int32, (ROWS, HD), 1)
        stat_ref[...] = jnp.where(lane == 0, top, jnp.where(lane == 1, total, weighted))


def stats_call(first, info, groups, rest, last=False):
    pieces = [piece for group in groups for piece in group]
    if first == 0:
        out = [SHAPE((ROWS, HD), jnp.bfloat16)] * 2 + STATE
    elif last:
        out = [SHAPE((ROWS, HD), jnp.float32)] + [SHAPE((KB, HD), jnp.bfloat16)] * 2
    else:
        out = STATE
    keys = len(groups) * KB
    scratch = [pltpu.VMEM((keys, HD), jnp.bfloat16)] * 2
    if last:
        scratch = [pltpu.VMEM((ROWS, HD), jnp.float32)] * 3 + scratch
    return pl.pallas_call(
        functools.partial(stats_kernel, first, [len(group) for group in groups], last),
        out_shape=out,
        in_specs=[SM] + [VM] * (len(pieces) + len(rest)),
        out_specs=[VM] * len(out),
        scratch_shapes=scratch,
        compiler_params=pltpu.CompilerParams(vmem_limit_bytes=VMEM_LIMIT),
        cost_estimate=block_cost(len(groups) + (1 if last else 0), 2),
        name="stats_" + str(first),
    )(info, *pieces, *rest)


def grad_block(scores, dprobs, mask, lse, delta):
    probs = []
    dscores = []
    for g in range(KB // HD):
        p = jnp.exp2(scores[:, head_cols(g)] * EXP_SCALE - lse)
        if mask is not None:
            p = jnp.where(mask[:, head_cols(g)], p, 0.0)
        probs.append(p.astype(jnp.bfloat16))
        dscores.append((p * (dprobs[:, head_cols(g)] - delta)).astype(jnp.bfloat16))
    return jnp.concatenate(probs, 1), jnp.concatenate(dscores, 1)


def window_kernel(
    info_ref, mine_ref, pair_ref, q_s, do_s, wk_ref, wv_ref, lse_ref, delta_ref, dq_ref, *rest
):
    parts, dkv_ref = rest[:4], rest[4]
    mine = mine_ref[...]
    half = ROWS // 2
    pair = jnp.concatenate([pair_ref[half:, :], pair_ref[:half, :]], 0)
    top = jnp.maximum(mine[:, 0:1], pair[:, 0:1])
    fix = jnp.exp2((mine[:, 0:1] - top) * EXP_SCALE)
    pair_fix = jnp.exp2((pair[:, 0:1] - top) * EXP_SCALE)
    total = mine[:, 1:2] * fix + pair[:, 1:2] * pair_fix
    weighted = mine[:, 2:3] * fix + pair[:, 2:3] * pair_fix
    lse_ref[...] = jnp.broadcast_to(top * EXP_SCALE + jnp.log2(total), (ROWS, HD))
    delta_ref[...] = jnp.broadcast_to(weighted / total, (ROWS, HD))
    dkv_ref[...] = jnp.zeros((KB, 2 * HD), jnp.float32)

    mask = window_mask(info_ref)
    keys = wk_ref[...]
    values = wv_ref[...]

    def dots(r):
        return contract_last(q_s[chunk(r), :], keys), contract_last(do_s[chunk(r), :], values)

    def rest(r, scores, dprobs):
        rows = chunk(r)
        probs, dscores = grad_block(scores, dprobs, mask, lse_ref[rows, :], delta_ref[rows, :])
        dq_ref[rows, :] = jnp.dot(dscores, keys, preferred_element_type=jnp.float32)
        dkv_ref[:, :HD] += contract_first(dscores, q_s[rows, :])
        dkv_ref[:, HD:] += contract_first(probs, do_s[rows, :])

    pipelined(dots, rest)

    for dz in range(4):
        at = pl.multiple_of(lax.bitwise_and(info_ref[Z] + dz, 3) * TOK, TOK)
        parts[dz][...] = dkv_ref[pl.ds(at, TOK), :]


def window_call(info, mine, pair, query, dout, win_k, win_v):
    out = STATE + [SHAPE((TOK, 2 * HD), jnp.float32)] * 4
    return pl.pallas_call(
        window_kernel,
        out_shape=out,
        in_specs=[SM] + [VM] * 6,
        out_specs=[VM] * 7,
        scratch_shapes=[pltpu.VMEM((KB, 2 * HD), jnp.float32)],
        compiler_params=pltpu.CompilerParams(vmem_limit_bytes=VMEM_LIMIT),
        cost_estimate=block_cost(1, 5),
        name="window_grads",
    )(info, mine, pair, query, dout, win_k, win_v)


def fetches(info_ref, weights, w_ref, kv_ref, sems):
    wq_ref, wk_ref, wv_ref, pair_wq_ref, pair_wk_ref, pair_wv_ref = weights
    copies = []
    for j in range(CHIPS):
        rows = pl.ds(pl.multiple_of((2 * j + info_ref[CORE]) * FEAT, FEAT), FEAT)
        for n, ref in enumerate((wq_ref, pair_wq_ref)):
            target = w_ref.at[j, :, pl.ds(n * COLS, COLS)]
            copies.append(pltpu.make_async_copy(ref.at[rows, :], target, sems.at[j, n]))
        for n, ref in enumerate((wk_ref, wv_ref, pair_wk_ref, pair_wv_ref)):
            target = kv_ref.at[j, pl.ds(n * SIDE, SIDE), :]
            copies.append(pltpu.make_async_copy(ref.at[:, rows], target, sems.at[j, 2 + n]))
    return copies


def cache_kernel(first, groups, info_ref, *refs):
    refs = list(refs)
    copies = []
    if first == 0:
        sems = refs.pop()
        weights = [refs.pop(0) for _ in range(6)]
        w_ref, kv_ref = refs[-4], refs[-3]
        del refs[-4:-2]
        copies = fetches(info_ref, weights, w_ref, kv_ref, sems)
    for copy in copies:
        copy.start()
    pieces = []
    for size in groups:
        pieces.append([refs.pop(0) for _ in range(size)])
    q_s, do_s, lse_ref, delta_ref, dq_in, dq_ref, k_s, v_s = refs
    place_cache(pieces, k_s, v_s)
    dq_ref[...] = dq_in[...]

    def body(n, start, masked):
        keys = k_s[keys_at(n), :]
        values = v_s[keys_at(n), :]
        mask = cache_mask(info_ref, start) if masked else None

        def dots(r):
            return contract_last(q_s[chunk(r), :], keys), contract_last(do_s[chunk(r), :], values)

        def rest(r, scores, dprobs):
            rows = chunk(r)
            _, dscores = grad_block(scores, dprobs, mask, lse_ref[rows, :], delta_ref[rows, :])
            dq_ref[rows, :] += jnp.dot(dscores, keys, preferred_element_type=jnp.float32)

        pipelined(dots, rest)

    cache_loop(info_ref, first, len(groups), info_ref[CORE], body)
    for copy in copies:
        copy.wait()


def cache_call(first, info, groups, query, dout, lse, delta, dq, weights=()):
    pieces = [piece for group in groups for piece in group]
    out = STATE[:1]
    scratch = [pltpu.VMEM((len(groups) * KB, HD), jnp.bfloat16)] * 2
    if weights:
        out = out + [
            SHAPE((CHIPS, FEAT, 2 * COLS), jnp.bfloat16),
            SHAPE((CHIPS, 2 * HD, FEAT), jnp.bfloat16),
        ]
        scratch = scratch + [pltpu.SemaphoreType.DMA((CHIPS, 6))]
    return pl.pallas_call(
        functools.partial(cache_kernel, first, [len(group) for group in groups]),
        out_shape=out,
        in_specs=[SM] + [HB] * len(weights) + [VM] * (len(pieces) + 5),
        out_specs=[VM] * len(out),
        scratch_shapes=scratch,
        compiler_params=pltpu.CompilerParams(vmem_limit_bytes=VMEM_LIMIT),
        cost_estimate=block_cost(len(groups), 3),
        name="cache_grads_" + str(first),
    )(info, *weights, *pieces, query, dout, lse, delta, dq)


def sum_kernel(info_ref, a_ref, b_ref, c_ref, d_ref, keep_ref, send_ref):
    total = (a_ref[...] + b_ref[...]) + (c_ref[...] + d_ref[...])
    first = info_ref[XH] == 0
    keep_ref[...] = jnp.where(first, total[:HALF_WIN, :], total[HALF_WIN:, :])
    send_ref[...] = jnp.where(first, total[HALF_WIN:, :], total[:HALF_WIN, :])


def sum_parts(info, parts):
    return pl.pallas_call(
        sum_kernel,
        out_shape=[SHAPE((HALF_WIN, 2 * HD), jnp.float32)] * 2,
        in_specs=[SM] + [VM] * 4,
        out_specs=[VM] * 2,
        compiler_params=SMALL,
        name="sum_parts",
    )(info, *parts)


def own_kv_kernel(idx_ref, keep_ref, other_ref, raw_ref, gain_ref, out_ref):
    total = keep_ref[...] + other_ref[...]
    raw = raw_ref[...].astype(jnp.float32)
    out_ref[:, :HD] = unit_back(raw, gain_ref[...], total[:, :HD] * SCALE).astype(jnp.bfloat16)
    out_ref[:, HD:] = total[:, HD:].astype(jnp.bfloat16)


def own_kv(idx, keep, other, k_raw, gain):
    def whole(i, idx):
        return (0, 0)

    return pl.pallas_call(
        own_kv_kernel,
        out_shape=SHAPE((HALF_WIN, 2 * HD), jnp.bfloat16),
        grid_spec=pltpu.PrefetchScalarGridSpec(
            num_scalar_prefetch=1,
            grid=(1,),
            in_specs=[
                pl.BlockSpec((HALF_WIN, 2 * HD), whole),
                pl.BlockSpec((HALF_WIN, 2 * HD), whole),
                pl.BlockSpec((HALF_WIN, HD), lambda i, idx: (idx[CORE], idx[CHIP])),
                pl.BlockSpec((1, HD), whole),
            ],
            out_specs=pl.BlockSpec((HALF_WIN, 2 * HD), whole),
        ),
        compiler_params=SMALL,
        name="own_kv",
    )(idx, keep, other, k_raw, gain)


def project_kernel(
    info_ref,
    dq_ref,
    pair_dq_ref,
    q_ref,
    pair_q_ref,
    gain_ref,
    kv_ref,
    pair_kv_ref,
    w_ref,
    wkv_ref,
    out_ref,
    g_s,
):
    core = info_ref[CORE]
    gain = gain_ref[...]
    for h in range(HEADS):
        rows = head_rows(h)
        low = slice(ROWS // 2 + h * TOK, ROWS // 2 + (h + 1) * TOK)
        for side, raw_ref, grad in (
            (0, q_ref, dq_ref[rows, :] + pair_dq_ref[low, :]),
            (1, pair_q_ref, dq_ref[low, :] + pair_dq_ref[rows, :]),
        ):
            raw = raw_ref[:, head_cols(h)].astype(jnp.float32)
            at = side * COLS + h * HD
            g_s[at : at + HD, :] = unit_back(raw, gain, grad * SCALE).T.astype(jnp.bfloat16)
    here = kv_ref[...].astype(jnp.float32)
    there = pair_kv_ref[...].astype(jnp.float32)
    top = jnp.where(core == 0, here, there)
    bottom = jnp.where(core == 0, there, here)
    kv = jnp.concatenate([top, bottom], 0)
    for n in range(2):
        both = kv[:, n * HD : (n + 1) * HD].T.astype(jnp.bfloat16)
        first = jnp.where(core == 0, both[:SIDE, :], both[SIDE:, :])
        second = jnp.where(core == 0, both[SIDE:, :], both[:SIDE, :])
        g_s[2 * COLS + n * SIDE : 2 * COLS + (n + 1) * SIDE, :] = first
        g_s[2 * COLS + (2 + n) * SIDE : 2 * COLS + (3 + n) * SIDE, :] = second
    for j in range(CHIPS):
        total = contract_first(wkv_ref[j], g_s[2 * COLS :, :])
        total += jnp.dot(w_ref[j], g_s[: 2 * COLS, :], preferred_element_type=jnp.float32)
        out_ref[j] = total.astype(jnp.bfloat16)


def project(info, *operands):
    return pl.pallas_call(
        project_kernel,
        out_shape=SHAPE((CHIPS, FEAT, TOK), jnp.bfloat16),
        in_specs=[SM] + [VM] * 9,
        out_specs=VM,
        scratch_shapes=[pltpu.VMEM((2 * COLS + 2 * HD, TOK), jnp.bfloat16)],
        compiler_params=pltpu.CompilerParams(vmem_limit_bytes=VMEM_LIMIT),
        cost_estimate=cost(2 * TOK * D // 2 * 1280, 0, 12e6),
        name="project",
    )(info, *operands)


def rows_kernel(pieces_ref, resid_ref, dh_ref, grad_ref, sums_ref):
    inner = jnp.zeros((1, TOK), jnp.float32)
    square = jnp.zeros((1, TOK), jnp.float32)
    for n in range(FEAT // HD):
        rows = head_cols(n)
        grad = pieces_ref[0, rows, :].astype(jnp.float32)
        for m in range(1, CHIPS):
            grad += pieces_ref[m, rows, :].astype(jnp.float32)
        grad += dh_ref[rows, :].astype(jnp.float32)
        grad_ref[rows, :] = grad
        resid = resid_ref[rows, :].astype(jnp.float32)
        inner += jnp.sum(grad * resid, axis=0, keepdims=True)
        square += jnp.sum(resid * resid, axis=0, keepdims=True)
    row = lax.broadcasted_iota(jnp.int32, (8, TOK), 0)
    sums_ref[...] = jnp.where(row == 0, inner, square)


def row_sums(pieces, resid_t, dh_t):
    return pl.pallas_call(
        rows_kernel,
        out_shape=[SHAPE((FEAT, TOK), jnp.float32), SHAPE((8, TOK), jnp.float32)],
        in_specs=[VM] * 3,
        out_specs=[VM] * 2,
        compiler_params=SMALL,
        name="row_sums",
    )(pieces, resid_t, dh_t)


def norm_kernel(grad_ref, sums_ref, resid_ref, out_ref):
    sums = sums_ref[0]
    for n in range(1, 2 * CHIPS):
        sums += sums_ref[n]
    mean_sq = sums[1:2, :] / D
    factor = lax.rsqrt(mean_sq + EPS) / math.sqrt(D)
    correction = sums[0:1, :] / (D * (mean_sq + EPS))
    for n in range(FEAT // HD):
        rows = head_cols(n)
        resid = resid_ref[rows, :].astype(jnp.float32)
        out_ref[:, rows] = (factor * (grad_ref[rows, :] - resid * correction)).T


def last_norm(grad_t, sums, resid_t):
    return pl.pallas_call(
        norm_kernel,
        out_shape=SHAPE((TOK, FEAT), jnp.float32),
        in_specs=[VM] * 3,
        out_specs=VM,
        compiler_params=SMALL,
        name="last_norm",
    )(grad_t, sums, resid_t)


def shift(block, axis, by):
    count = lax.axis_size(axis)
    return lax.ppermute(block, axis, [(i, (i + by) % count) for i in range(count)])


def swap(block, axis):
    return shift(block, axis, 1)


def on_device(
    residual_in,
    dh_rest,
    w_query,
    w_key,
    w_value,
    q_raw,
    k_raw,
    v_win,
    cache_k,
    cache_v,
    d_attn,
    s_qk,
    cache_live,
):
    info = jnp.stack(
        [
            lax.axis_index("z"),
            lax.axis_index("xh"),
            lax.axis_index("xl") * 4 + lax.axis_index("y"),
            lax.axis_index("c"),
            CACHE - cache_live[0],
        ]
    ).astype(jnp.int32)
    sources = [cache_k, cache_v, k_raw, v_win, residual_in, dh_rest, q_raw, d_attn]
    sources.append(s_qk.reshape(1, HD))
    sources = [pltpu.with_memory_space_constraint(array, pltpu.HBM) for array in sources]
    here, resid_t, dh_t, q_own, do_own, gain = pack_rows(info, *sources)
    there = swap(here, "xh")
    up = shift(here, "z", -1)
    down = shift(here, "z", 1)
    pair_wide = swap(w_query, "c")
    there, late_q, late_do = lax.optimization_barrier((there, q_own, do_own))
    pair_q = swap(late_q, "c")
    pair_do = swap(late_do, "c")
    up_there = shift(there, "z", -1)
    down_there = shift(there, "z", 1)
    far = shift(up, "z", -1)
    groups = [[here], [there], [up], [down]]
    narrow = [w_key.T, w_value.T]
    narrow, pair_do, pair_wide = lax.optimization_barrier((narrow, pair_do, pair_wide))
    pair_weights = [pair_wide] + [swap(w, "c") for w in narrow]
    query, dout, *state = stats_call(
        0, info, groups[:4], [q_own, do_own, pair_q, pair_do, gain]
    )
    far_there = shift(down_there, "z", 1)
    groups += [[up_there], [down_there], [far], [far_there]]
    state = stats_call(4, info, groups[4:6], [query, dout, *state])
    wins = [group[-1] for group in groups[:6]]
    stat, win_k, win_v = stats_call(
        6, info, groups[6:], wins + [query, dout, *state], last=True
    )
    weights = [pltpu.with_memory_space_constraint(w_query, pltpu.HBM), *narrow]
    pair_stat, pair_weights = lax.optimization_barrier((swap(stat, "c"), pair_weights))
    lse, delta, dq, *parts = window_call(info, stat, pair_stat, query, dout, win_k, win_v)
    parts = [parts[0]] + [shift(parts[dz], "z", dz) for dz in (1, 3, 2)]
    dq, w_own, w_kv = cache_call(
        0, info, groups[:6], query, dout, lse, delta, dq, [*weights, *pair_weights]
    )
    parts, dq = lax.optimization_barrier((parts, dq))
    keep, send = sum_parts(info, parts)
    other = swap(send, "xh")
    (dq,) = cache_call(6, info, groups[6:], query, dout, lse, delta, dq)
    other, dq = lax.optimization_barrier((other, dq))
    pair_dq = swap(dq, "c")
    kv = own_kv(info, keep, other, k_raw, gain)
    pair_kv = swap(kv, "c")
    partial = project(info, dq, pair_dq, q_own, pair_q, gain, kv, pair_kv, w_own, w_kv)
    pieces = lax.all_to_all(partial, CHIP_AXES, 0, 0)
    grad_t, sums = row_sums(pieces, resid_t, dh_t)
    everyone = lax.all_to_all(
        jnp.broadcast_to(sums[None], (2 * CHIPS, 8, TOK)), TP_AXES, 0, 0
    )
    return last_norm(grad_t, everyone, resid_t)


def solution(mesh):
    fine = Mesh(mesh.devices.reshape(4, 2, 2, 4, 2), ("z", "xh", "xl", "y", "c"))
    both = P(CTX_AXES, TP_AXES)
    cols = P(None, TP_AXES)
    rows = P(CTX_AXES, None)
    return jax.shard_map(
        on_device,
        mesh=fine,
        in_specs=(both, both, cols, cols, cols, both, rows, rows, rows, rows, both, P(), P()),
        out_specs=both,
        check_vma=False,
    )
```
